256 devices in a mesh: mod: 64 (over x, z, core), tp: 4 (over y).
Axes of the slice: x: 4, y: 4, z: 8, core: 2. Of those that a mesh axis runs over, the one named last changes fastest.
Arguments:
- stream: bfloat16 [49152, 4096], P('mod'), as said below
- norm_gain: float32 [2, 4096], replicated, may hold values from 0.1 to 1.9
- qkv_weight: bfloat16 [2, 4096, 3, 2048], P(None, 'mod', None, 'tp'), may hold values from -0.09375 to 0.09375
- qk_gain: float32 [2, 2, 2048], P(None, None, 'tp'), may hold values from 0.6 to 2.5
- owner: int32 [32768], replicated, may hold values from 0 to 63, as said below
- doc_lengths: int32 [8, 4], replicated, may hold values from 1 to 2048, 4096 in all within a row
Outputs:
- context: bfloat16 [49152, 2048], P('mod', 'tp')
The draws below stay inside these ranges and needn't reach their ends.
Inputs may be any that keep to these rules, and one draw needn't show every extreme that they name: `owner`: owners below 32 form the text section, the others the image section. In each aligned block of 256 tokens the text tokens form one contiguous run of 64 tokens; every text section device owns exactly 2 of them and every image section device exactly 6 of the image tokens of that block. Rows of stream that no token's slot names are never read.
All inputs are finite; a program needn't handle non-finite values.
Results may differ from the reference program's by a relative error of at most 0.011.
Values may be sent and summed in bfloat16 or wider, within the bound.
A program may use at most 128 MiB of HBM per device.

```python
import math
import jax
import jax.numpy as jnp
import numpy as np
from jax import lax

D = 4096
HEADS = 16
HD = 128
TOK_DEV = 512
SEQ_DEVS = 8
DOCS = 4
SEQ_LEN = 4096
SEQS = 8
TOKENS = 32768
TEXT_DEVS = 32
ROWS_DEV = 768
SLOTS = 49152
N_MOD = 64


def draw_owner(key, part):
    half_len = TOK_DEV // 2
    run_len = TOK_DEV // 8
    image_len = half_len - run_len
    block_count = TOKENS // half_len
    base = jax.random.fold_in(key, 11)
    key_start = jax.random.fold_in(base, 1)
    key_text = jax.random.fold_in(base, 2)
    key_image = jax.random.fold_in(base, 3)
    starts = jax.random.randint(key_start, (block_count, 1), 0, image_len + 1)
    within = jnp.arange(half_len, dtype=jnp.int32)[None, :]
    is_text = (within >= starts) & (within < starts + run_len)
    text_rank = jnp.cumsum(is_text.astype(jnp.int32), axis=1) - 1
    image_rank = jnp.cumsum(1 - is_text.astype(jnp.int32), axis=1) - 1
    text_order = jax.vmap(lambda subkey: jax.random.permutation(subkey, run_len))(jax.random.split(key_text, block_count))
    image_order = jax.vmap(lambda subkey: jax.random.permutation(subkey, image_len))(jax.random.split(key_image, block_count))
    text_owner = jnp.take_along_axis(text_order, jnp.clip(text_rank, 0, run_len - 1), axis=1) % TEXT_DEVS
    image_owner = TEXT_DEVS + jnp.take_along_axis(image_order, jnp.clip(image_rank, 0, image_len - 1), axis=1) % TEXT_DEVS
    return jnp.where(is_text, text_owner, image_owner).reshape(-1).astype(jnp.int32)


def draw_stream(key, part):
    base = jax.random.fold_in(key, 23)
    key_body = jax.random.fold_in(base, 1)
    key_rows = jax.random.fold_in(base, 2)
    key_cols = jax.random.fold_in(base, 3)
    row_scale = jnp.exp(jax.random.uniform(key_rows, (SLOTS, 1), minval=0.0, maxval=math.log(10.0)))
    col_scale = jnp.exp(jax.random.uniform(key_cols, (1, D), minval=0.0, maxval=math.log(10.0)))
    body_part = jax.random.normal(key_body, (SLOTS, D))
    return (body_part * row_scale * col_scale / 3.0).astype(jnp.bfloat16)


def block_scale(rng, dims, cuts, low, high):
    loudness, own = 1.0, jax.random.fold_in(rng, 6)
    for position, shards_of in cuts:
        draws = jnp.exp(jax.random.uniform(jax.random.fold_in(own, position), (shards_of,), jnp.float32, low / len(cuts), high / len(cuts)))
        loudness = loudness * jnp.repeat(draws, dims[position] // shards_of).reshape([-1 if axis == position else 1 for axis in range(len(dims))])
    return loudness


def split_up(number_of, total, bound, slope):
    loads = [(1 << 20) // math.isqrt(grade ** slope) + 1 for grade in range(2, number_of + 1)]
    surplus, given = total - bound - (number_of - 1), [1] * (number_of - 1)
    while surplus > 0:
        free = [i for i in range(number_of - 1) if given[i] < bound]
        pool, remaining = sum([loads[i] for i in free]), surplus
        for i in free:
            extra = min(bound - given[i], max(1, remaining * loads[i] // pool), surplus)
            given[i] = given[i] + extra
            surplus = surplus - extra
    return np.array([bound] + given)


def uneven_parts(key, amount, total, bound, slope):
    if amount == 2:
        one = jax.random.randint(key, (), max(1, total - bound), min(bound, total - 1) + 1)
        return jnp.stack([one, total - one])
    sizes = jnp.asarray(split_up(amount, total, bound, slope), jnp.int32)
    pairs = (amount - 1) // 2
    donor, receiver = sizes[1:1 + 2 * pairs:2], sizes[2:2 + 2 * pairs:2]
    slack = jnp.minimum(donor - 1, bound - receiver)
    moved = jax.random.randint(jax.random.fold_in(key, 1), (pairs,), 0, 1 << 20) % (slack + 1)
    sizes = sizes.at[1:1 + 2 * pairs:2].set(donor - moved).at[2:2 + 2 * pairs:2].set(receiver + moved)
    return sizes[jax.random.permutation(jax.random.fold_in(key, 2), amount)]


def noise(stream_key, dims, scale, bound, cuts=(), kind=jnp.bfloat16):
    drawn = jax.random.normal(stream_key, dims, jnp.float32) * scale
    if len(cuts) > 0:
        drawn = block_scale(stream_key, dims, cuts, -0.22, 0.18) * drawn
    return jnp.clip(drawn, min=-bound, max=bound).astype(kind)


def setup_inputs(seed: int = 0) -> dict:
    keys = jax.random.split(jax.random.key(seed), 7)
    return {
        "stream": draw_stream(jax.random.fold_in(keys[6], 71), 0),
        "norm_gain": jnp.clip(1.0 + 0.18 * jax.random.normal(keys[1], (2, D), jnp.float32), 0.1, 1.9),
        "qkv_weight": noise(keys[2], (2, D, 3, HEADS * HD), D ** -0.5, 0.09375, ((1, 64), (3, 4))),
        "qk_gain": jnp.clip(jnp.exp(math.log(2.5) - 1.4271163 * jax.random.uniform(keys[3], (2, 2, HEADS * HD), jnp.float32) ** block_scale(keys[3], (2, 2, HEADS * HD), ((2, 4),), -0.2, 0.2)), 0.6, 2.5),
        "owner": draw_owner(jax.random.fold_in(keys[6], 71), 0),
        "doc_lengths": jax.vmap(lambda own: uneven_parts(own, DOCS, SEQ_LEN, SEQ_LEN // 2, 1))(jax.random.split(keys[5], SEQS)).reshape((SEQS, DOCS)).astype(jnp.int32),
    }


epsilon = 1e-05
rope_base = 10000.0

def head_norm(values, scales):
    centre = lax.optimization_barrier(jnp.mean(values, axis=-1, keepdims=True))
    centred = values - centre
    spread = lax.optimization_barrier(jnp.mean(centred * centred, axis=-1, keepdims=True))
    return centred * lax.rsqrt(spread + epsilon) * scales

def rotary(values, places):
    half_dim = values.shape[-1] // 2
    freqs = jnp.exp(-math.log(rope_base) * 2.0 * jnp.arange(half_dim, dtype=jnp.float32) / values.shape[-1])
    angles = places.astype(jnp.float32)[:, None] * freqs[None, :]
    cosine = jnp.cos(angles)[:, None, :]
    sine_part = jnp.sin(angles)[:, None, :]
    front = values[..., :half_dim]
    back = values[..., half_dim:]
    return jnp.concatenate([front * cosine - back * sine_part, back * cosine + front * sine_part], axis=-1)

def doc_info(doc_lengths, tokens):
    seq_len = SEQ_DEVS * TOK_DEV
    lengths = doc_lengths.reshape(-1).astype(jnp.int32)
    labels = jnp.arange(lengths.shape[0], dtype=jnp.int32)
    ends = labels // DOCS * seq_len + jnp.cumsum(doc_lengths, axis=1).astype(jnp.int32).reshape(-1)
    starts = ends - lengths
    inside = (tokens[:, None] >= starts[None, :]) & (tokens[:, None] < ends[None, :])
    doc_ids = lax.optimization_barrier(jnp.sum(jnp.where(inside, labels[None, :], 0), axis=1)).astype(jnp.int32)
    first_tok = lax.optimization_barrier(jnp.sum(jnp.where(inside, starts[None, :], 0), axis=1)).astype(jnp.int32)
    return (doc_ids, (tokens - first_tok).astype(jnp.int32))

def attend(item):
    rows, docs = item
    length = docs.shape[0]
    block = min(512, length)
    key_rows = rows[:, 1].astype(jnp.float32)
    values = rows[:, 2].astype(jnp.float32)
    order = jnp.arange(length, dtype=jnp.int32)
    query_blocks = rows[:, 0].reshape(length // block, block, HEADS, HD)
    doc_blocks = docs.reshape(length // block, block)
    order_blocks = order.reshape(length // block, block)

    def one_block(piece):
        queries, query_docs, query_order = piece
        scores = jnp.einsum('qhd,khd->hqk', queries.astype(jnp.float32), key_rows) / math.sqrt(HD)
        visible = (query_docs[:, None] == docs[None, :]) & (order[None, :] <= query_order[:, None])
        weights = jnp.where(visible[None], jnp.exp(scores), 0.0)
        rounded = lax.optimization_barrier(weights.astype(jnp.bfloat16)).astype(jnp.float32)
        numerator = jnp.einsum('hqk,khd->qhd', rounded, values)
        denominator = lax.optimization_barrier(jnp.sum(weights, axis=2))
        mixed = numerator / jnp.transpose(denominator)[:, :, None]
        return mixed.astype(jnp.bfloat16).reshape(block, HEADS * HD)
    return lax.map(one_block, (query_blocks, doc_blocks, order_blocks)).reshape(length, HEADS * HD)

def reference(stream, norm_gain, qkv_weight, qk_gain, owner, doc_lengths):
    tokens = jnp.arange(TOKENS, dtype=jnp.int32)
    doc_ids, places = doc_info(doc_lengths, tokens)
    picks = (owner[:, None] == jnp.arange(N_MOD, dtype=jnp.int32)[None, :]).astype(jnp.int32)
    earlier = jnp.cumsum(picks, axis=0).astype(jnp.int32) - picks
    slot = (owner * ROWS_DEV + lax.optimization_barrier(jnp.sum(earlier * picks, axis=1))).astype(jnp.int32)
    slot_places = jnp.zeros((SLOTS,), jnp.int32).at[slot].set(places).reshape(N_MOD, ROWS_DEV)
    blocks = stream.reshape(N_MOD, ROWS_DEV, D)
    text_rows = TOK_DEV // 2
    width = HEADS * HD

    def project(rows, modality, row_places):
        sample = rows.astype(jnp.float32)
        normed = (sample * lax.rsqrt(lax.optimization_barrier(jnp.mean(sample * sample, axis=1, keepdims=True)) + epsilon) * norm_gain[modality]).astype(jnp.bfloat16)
        projected = jnp.dot(normed, qkv_weight[modality].reshape(D, 3 * width), preferred_element_type=jnp.float32)
        projected = projected.reshape(-1, 3, HEADS, HD)
        scales = qk_gain[modality].reshape(2, HEADS, HD)
        queries = rotary(head_norm(projected[:, 0], scales[0]), row_places)
        rotated_keys = rotary(head_norm(projected[:, 1], scales[1]), row_places)
        return jnp.stack([queries, rotated_keys, projected[:, 2]], axis=1).astype(jnp.bfloat16)
    text_out = project(blocks[:TEXT_DEVS, :text_rows].reshape(-1, D), 0, slot_places[:TEXT_DEVS, :text_rows].reshape(-1))
    text_out = jnp.pad(text_out.reshape(TEXT_DEVS, text_rows, 3, width), ((0, 0), (0, ROWS_DEV - text_rows), (0, 0), (0, 0)))
    image_out = project(blocks[TEXT_DEVS:].reshape(-1, D), 1, slot_places[TEXT_DEVS:].reshape(-1))
    image_out = image_out.reshape(N_MOD - TEXT_DEVS, ROWS_DEV, 3, width)
    by_slot = jnp.concatenate([text_out, image_out], axis=0).reshape(SLOTS, 3, width)
    in_order = by_slot[slot].reshape(SEQS, SEQ_LEN, 3, HEADS, HD)
    docs_in_order = doc_ids.reshape(SEQS, SEQ_LEN)
    mixed = lax.map(attend, (in_order, docs_in_order)).reshape(TOKENS, width)
    return jnp.zeros((SLOTS, width), jnp.bfloat16).at[slot].set(mixed)
```

```python
import math

import jax
import jax.numpy as jnp
import numpy as np
from jax import lax
from jax.experimental import pallas as pl
from jax.experimental.pallas import tpu as pltpu
from jax.sharding import PartitionSpec as P

HD = 128
BLOCK = 256
SEQ_LEN = 4096
SEQS = 8
BLOCKS = 128
ROWS = 768
TEXT_ROWS = 256
XS = 4
ZS = 8
CHIPS = XS * ZS
HEADS = 4
WIDTH = HEADS * HD
MODEL = 4096
K_CHUNK = 64
TEXT_CHIPS = CHIPS // 2
TEXT_HALF = 16
IMAGE_HALF = 48
PART = TEXT_CHIPS * (TEXT_HALF + IMAGE_HALF)
Q_TILE = 256
MESH = pl.DeviceIdType.MESH

epsilon = 1e-05
rope_base = 10000.0


def place_of():
    me = lax.axis_index("mod")
    core = lax.rem(me, 2)
    chip = lax.div(me, 2)
    return lax.div(chip, ZS), lax.rem(chip, ZS), core, lax.axis_index("tp")


def project_kernel(
    w_ref, x_ref, gain_ref, cos_ref, sin_ref, qk_ref, out_ref,
    weights, rows, normed, acc,
    z_send, z_recv, x_send, x_recv, s_send, s_recv, c_send, c_recv, load_sem, own_sem,
):
    x, z, core, tp = place_of()
    modality = lax.div(x, 2)
    x_in = x + 1 - 2 * lax.rem(x, 2)
    columns = (x, 3 - x, 3 - x_in)

    def device(xx, zz, cc):
        return ((xx * ZS + zz) * 2 + cc, tp)

    def around(steps):
        return lax.rem(z + steps + 2 * ZS, ZS)

    z_next = (device(x, around(1), core), device(x, around(-1), core))
    partner = device(x_in, z, core)
    across = device(3 - x, z, core)
    sibling = device(x, z, 1 - core)

    def put(src, dst, send, recv, target):
        return pltpu.make_async_remote_copy(
            src_ref=src, dst_ref=dst, send_sem=send, recv_sem=recv,
            device_id=target, device_id_type=MESH,
        )

    def spot(zz, xx):
        return weights.at[zz, :, xx, core]

    def along_z(kind, way, hop, src=None):
        zz = around((1 - hop) if way == 0 else (hop - 1))
        here = spot(zz, columns[kind])
        return put(
            here if src is None else src, here,
            z_send.at[kind, way, hop - 1], z_recv.at[kind, way, hop - 1], z_next[way],
        )

    def to_partner(slot, zz, xx, src=None):
        here = spot(zz, xx)
        return put(here if src is None else src, here, x_send.at[slot], x_recv.at[slot], partner)

    def to_sibling(zz, xx, src=None):
        here = spot(zz, xx)
        return put(
            here if src is None else src, here, s_send.at[zz, xx], s_recv.at[zz, xx], sibling
        )

    def long_way(kind):
        return lax.rem(kind + core, 2)

    barrier = pltpu.get_barrier_semaphore()
    for target in (z_next[0], z_next[1], partner, across, sibling):
        pl.semaphore_signal(barrier, inc=1, device_id=target, device_id_type=MESH)
    pl.semaphore_wait(barrier, 5)

    mine = w_ref.at[modality]
    cross = put(w_ref.at[1 - modality], spot(z, x), c_send, c_recv, across)
    cross.start()
    for way in range(2):
        along_z(0, way, 1, mine).start()
    to_partner(z, z, x, mine).start()
    to_sibling(z, x, mine).start()
    own = pltpu.make_async_copy(mine, spot(z, x), own_sem)
    own.start()
    pieces = [
        pltpu.make_async_copy(
            x_ref.at[pl.ds(i * 128, 128)], rows.at[pl.ds(i * 128, 128)], load_sem.at[i]
        )
        for i in range(ROWS // 128)
    ]
    for piece in pieces:
        piece.start()

    def normalize(i):
        pieces[i].wait()

        @pl.loop(0, 8)
        def _(group):
            at = pl.multiple_of(i * 128 + group * 16, 16)
            sample = rows[pl.ds(at, 16), :].astype(jnp.float32)
            scale = lax.rsqrt(jnp.mean(sample * sample, axis=1, keepdims=True) + epsilon)
            scaled = (sample * scale * gain_ref[pl.ds(modality, 1), :]).astype(jnp.bfloat16)
            for zz in range(ZS):
                for xx in range(XS):
                    k = (xx * ZS + zz) * 128
                    normed[zz, pl.ds(at, 16), xx * 128 : xx * 128 + 128] = scaled[:, k : k + 128]

    normalize(0)
    normalize(1)
    put(w_ref.at[modality], spot(z, 3 - x), c_send, c_recv, across).wait_recv()
    to_partner(ZS, z, 3 - x).start()
    for way in range(2):
        along_z(1, way, 1).start()
    to_sibling(z, 3 - x).start()
    normalize(2)
    normalize(3)
    to_partner(ZS, z, 3 - x_in).wait_recv()
    for way in range(2):
        along_z(2, way, 1).start()
    to_sibling(z, 3 - x_in).start()
    to_partner(z, z, x_in).wait_recv()
    to_sibling(z, x_in).start()
    normalize(4)
    normalize(5)
    own.wait()

    def arrive(kind, way, hop, last):
        zz = around(-hop if way == 0 else hop)
        along_z(kind, way, hop).wait_recv()
        if not last:
            onward = jnp.logical_or(hop < 3, long_way(kind) == way)

            @pl.when(onward)
            def _():
                along_z(kind, way, hop + 1).start()

        if kind == 0:
            to_partner(zz, zz, x).start()
        to_sibling(zz, columns[kind]).start()

    def from_partner(zz):
        to_partner(zz, zz, x_in).wait_recv()
        to_sibling(zz, x_in).start()

    def consume(zz, first=False):
        for xx in range(XS):
            to_sibling(zz, xx).wait_recv()
        lhs = normed[zz]
        for j in range(3):
            part = jnp.dot(
                lhs, weights[zz, j].reshape(XS * 2 * K_CHUNK, WIDTH),
                preferred_element_type=jnp.float32,
            )
            if first:
                acc[j] = part
            else:
                acc[j] += part

    def hop_step(hop, first):
        for kind in range(3):
            for way in range(2):
                arrive(kind, way, hop, False)
        for way in range(2):
            from_partner(around(-hop if way == 0 else hop))
        if first:
            consume(z, True)

    hop_step(1, True)

    @pl.loop(2, 4)
    def _(hop):
        hop_step(hop, False)

        @pl.loop(0, 2)
        def _(way):
            consume(around((hop - 1) * (2 * way - 1)))

    @pl.loop(0, 2)
    def _(way):
        consume(around(3 * (2 * way - 1)))

    far = around(4)
    for kind in range(3):
        for way in range(2):

            @pl.when(long_way(kind) == way)
            def _():
                arrive(kind, way, 4, True)

    from_partner(far)
    consume(far)

    @pl.loop(0, ROWS // 128)
    def _(i):
        at = pl.ds(pl.multiple_of(i * 128, 128), 128)
        cosine = cos_ref[at, :]
        sine = sin_ref[at, :]
        for head in range(HEADS):
            lanes = slice(head * HD, head * HD + HD)
            for j in range(2):
                value = acc[j, at, lanes]
                centred = value - jnp.mean(value, axis=-1, keepdims=True)
                spread = jnp.mean(centred * centred, axis=-1, keepdims=True)
                scaled = centred * lax.rsqrt(spread + epsilon) * qk_ref[modality, pl.ds(j, 1), lanes]
                turned = scaled * cosine + pltpu.roll(scaled, HD // 2, 1) * sine
                out_ref[head, j, at, :] = turned.astype(jnp.bfloat16)
            out_ref[head, 2, at, :] = acc[2, at, lanes].astype(jnp.bfloat16)

    cross.wait_send()
    for kind in range(3):
        for way in range(2):
            for hop in range(1, 4):
                along_z(kind, way, hop).wait_send()

            @pl.when(long_way(kind) == way)
            def _():
                along_z(kind, way, 4).wait_send()

    for slot in range(ZS):
        to_partner(slot, slot, x).wait_send()
    to_partner(ZS, z, x).wait_send()
    for zz in range(ZS):
        for xx in range(XS):
            to_sibling(zz, xx).wait_send()


def project(w, stream, gain, cosines, sines, qk):
    vmem = pl.BlockSpec(memory_space=pltpu.VMEM)
    dma = pltpu.SemaphoreType.DMA
    return pl.pallas_call(
        project_kernel,
        name="gather_project",
        out_shape=jax.ShapeDtypeStruct((HEADS, 3, ROWS, HD), jnp.bfloat16),
        in_specs=[vmem, pl.BlockSpec(memory_space=pl.ANY), vmem, vmem, vmem, vmem],
        out_specs=vmem,
        scratch_shapes=[
            pltpu.VMEM((ZS, 3, XS, 2, K_CHUNK, WIDTH), jnp.bfloat16),
            pltpu.VMEM((ROWS, MODEL), jnp.bfloat16),
            pltpu.VMEM((ZS, ROWS, XS * 128), jnp.bfloat16),
            pltpu.VMEM((3, ROWS, WIDTH), jnp.float32),
            dma((3, 2, 4)), dma((3, 2, 4)),
            dma((ZS + 1,)), dma((ZS + 1,)),
            dma((ZS, XS)), dma((ZS, XS)),
            dma, dma,
            dma((ROWS // 128,)), dma,
        ],
        compiler_params=pltpu.CompilerParams(
            collective_id=0, has_side_effects=True, vmem_limit_bytes=60 << 20
        ),
    )(w, stream, gain, cosines, sines, qk)


def attend_kernel(
    pay_ref, kpos_ref, qpos_ref, qstart_ref, out_ref,
    held, num, den, mixed, blank,
    a_send, a_recv, s_send, s_recv, b_send, b_recv, zero_sem,
):
    x, z, core, tp = place_of()
    me = x * ZS + z
    seq, head = lax.div(me, HEADS), lax.rem(me, HEADS)
    is_image = x >= XS // 2
    sibling = (2 * me + 1 - core, tp)

    def chip(steps):
        return lax.rem(me + steps + CHIPS, CHIPS)

    barrier = pltpu.get_barrier_semaphore()

    @pl.loop(1, CHIPS)
    def _(i):
        pl.semaphore_signal(
            barrier, inc=1, device_id=(2 * chip(i) + core, tp), device_id_type=MESH
        )

    pl.semaphore_signal(barrier, inc=1, device_id=sibling, device_id_type=MESH)
    pl.semaphore_wait(barrier, CHIPS)

    def outbound(to, image, part):
        size = IMAGE_HALF if image else TEXT_HALF
        at = pl.multiple_of((2 * lax.div(to, HEADS) + part) * size, 16)
        return pay_ref.at[lax.rem(to, HEADS), :, pl.ds(at, size)]

    def landing(source, image, part):
        if image:
            at = TEXT_CHIPS * TEXT_HALF + (source - TEXT_CHIPS) * IMAGE_HALF
            size = IMAGE_HALF
        else:
            at = source * TEXT_HALF
            size = TEXT_HALF
        return pl.ds(pl.multiple_of(at, 16), size)

    def forth(to, image, part, target):
        return pltpu.make_async_remote_copy(
            src_ref=outbound(to, image, part),
            dst_ref=held.at[:, part, core, landing(me, image, part)],
            send_sem=a_send.at[to], recv_sem=a_recv.at[me],
            device_id=target, device_id_type=MESH,
        )

    def both(test, do):
        @pl.when(test)
        def _():
            do(True)

        @pl.when(jnp.logical_not(test))
        def _():
            do(False)

    def start_self(image):
        for part in range(2):
            pltpu.make_async_copy(
                outbound(me, image, part),
                held.at[:, part, core, landing(me, image, part)],
                a_recv.at[me],
            ).start()

    both(is_image, start_self)

    @pl.loop(1, CHIPS)
    def _(i):
        to = chip(i)

        def start(image):
            for part in range(2):
                forth(to, image, part, (2 * to + core, tp)).start()

        both(is_image, start)

    @pl.when(jnp.logical_not(is_image))
    def _():
        blank[...] = jnp.zeros_like(blank)
        pltpu.make_async_copy(blank, out_ref.at[pl.ds(TEXT_ROWS, ROWS - TEXT_ROWS)], zero_sem).start()

    @pl.loop(0, CHIPS)
    def _(i):
        source = chip(-i)

        def arrive(image):
            size = 2 * (IMAGE_HALF if image else TEXT_HALF)
            whole = pay_ref.at[0, :, pl.ds(0, size)]
            pltpu.make_async_copy(whole, whole, a_recv.at[source]).wait()

        both(source >= TEXT_CHIPS, arrive)

    def share(part):
        mine = held.at[pl.ds(1, 2), part, core]
        return pltpu.make_async_remote_copy(
            src_ref=mine, dst_ref=mine, send_sem=s_send.at[part], recv_sem=s_recv.at[part],
            device_id=sibling, device_id_type=MESH,
        )

    def shared(part):
        other = held.at[pl.ds(1, 2), part, 1 - core]
        return pltpu.make_async_remote_copy(
            src_ref=other, dst_ref=other, send_sem=s_send.at[part], recv_sem=s_recv.at[part],
            device_id=sibling, device_id_type=MESH,
        )

    share(0).start()
    share(1).start()

    def attend(side, first):
        @pl.loop(0, 2 * PART // Q_TILE)
        def _(tile):
            part = lax.div(tile, PART // Q_TILE)
            at = pl.ds(
                pl.multiple_of(lax.rem(tile, PART // Q_TILE) * Q_TILE, Q_TILE), Q_TILE
            )
            query = held[0, part, core, at, :]
            place = qpos_ref[part, at, :]
            start = qstart_ref[part, at, :]

            def step(key_part, fresh):
                keys = held[1, key_part, side]
                values = held[2, key_part, side]
                scores = lax.dot_general(
                    query, keys, (((1,), (1,)), ((), ())), preferred_element_type=jnp.float32
                )
                spots = kpos_ref[key_part, side]
                visible = (spots <= place) & (spots >= start)
                weight = jnp.where(visible, jnp.exp(scores * (1.0 / math.sqrt(HD))), 0.0)
                total = jnp.sum(weight, axis=1, keepdims=True)
                product = jnp.dot(
                    weight.astype(jnp.bfloat16), values, preferred_element_type=jnp.float32
                )
                if fresh:
                    num[part, at, :] = product
                    den[part, at, :] = jnp.broadcast_to(total, product.shape)
                else:
                    num[part, at, :] += product
                    den[part, at, :] += jnp.broadcast_to(total, product.shape)

            step(0, first)

            @pl.when(part == 1)
            def _():
                step(1, False)

    attend(core, True)
    shared(0).wait_recv()
    shared(1).wait_recv()
    attend(1 - core, False)

    @pl.loop(0, 2 * PART // Q_TILE)
    def _(tile):
        part = lax.div(tile, PART // Q_TILE)
        at = pl.ds(pl.multiple_of(lax.rem(tile, PART // Q_TILE) * Q_TILE, Q_TILE), Q_TILE)
        mixed[part, at, :] = (num[part, at, :] / den[part, at, :]).astype(jnp.bfloat16)

    def home(image, part, who_seq, who_head):
        size = IMAGE_HALF if image else TEXT_HALF
        at = pl.multiple_of((2 * who_seq + part) * size, 16)
        return out_ref.at[pl.ds(at, size), pl.ds(pl.multiple_of(who_head * HD, HD), HD)]

    def back(to, image, part):
        return pltpu.make_async_remote_copy(
            src_ref=mixed.at[part, landing(to, image, part)],
            dst_ref=home(image, part, seq, head),
            send_sem=b_send.at[to], recv_sem=b_recv.at[me],
            device_id=(2 * to + core, tp), device_id_type=MESH,
        )

    @pl.loop(1, CHIPS)
    def _(i):
        to = chip(i)

        def start(image):
            for part in range(2):
                back(to, image, part).start()

        both(to >= TEXT_CHIPS, start)

    def back_self(image):
        for part in range(2):
            pltpu.make_async_copy(
                mixed.at[part, landing(me, image, part)],
                home(image, part, seq, head), b_recv.at[me],
            ).start()

    both(is_image, back_self)

    @pl.loop(0, CHIPS)
    def _(i):
        source = chip(-i)

        def arrive(image):
            size = 2 * (IMAGE_HALF if image else TEXT_HALF)
            whole = mixed.at[0, pl.ds(0, size)]
            pltpu.make_async_copy(whole, whole, b_recv.at[source]).wait()

        both(is_image, arrive)

    @pl.loop(1, CHIPS)
    def _(i):
        to = chip(i)

        def sent(image):
            size = 2 * (IMAGE_HALF if image else TEXT_HALF)
            whole = pay_ref.at[0, :, pl.ds(0, size)]
            pltpu.make_async_copy(whole, whole, a_send.at[to]).wait()

        both(is_image, sent)

        def returned(image):
            size = 2 * (IMAGE_HALF if image else TEXT_HALF)
            whole = mixed.at[0, pl.ds(0, size)]
            pltpu.make_async_copy(whole, whole, b_send.at[to]).wait()

        both(to >= TEXT_CHIPS, returned)

    share(0).wait_send()
    share(1).wait_send()

    @pl.when(jnp.logical_not(is_image))
    def _():
        pltpu.make_async_copy(blank, out_ref.at[pl.ds(TEXT_ROWS, ROWS - TEXT_ROWS)], zero_sem).wait()


def attend_all(payload, key_places, query_places, query_starts):
    vmem = pl.BlockSpec(memory_space=pltpu.VMEM)
    dma = pltpu.SemaphoreType.DMA
    return pl.pallas_call(
        attend_kernel,
        name="exchange_attend",
        out_shape=jax.ShapeDtypeStruct((ROWS, WIDTH), jnp.bfloat16),
        in_specs=[vmem, vmem, vmem, vmem],
        out_specs=pl.BlockSpec(memory_space=pl.ANY),
        scratch_shapes=[
            pltpu.VMEM((3, 2, 2, PART, HD), jnp.bfloat16),
            pltpu.VMEM((2, PART, HD), jnp.float32),
            pltpu.VMEM((2, PART, HD), jnp.float32),
            pltpu.VMEM((2, PART, HD), jnp.bfloat16),
            pltpu.VMEM((ROWS - TEXT_ROWS, WIDTH), jnp.bfloat16),
            dma((CHIPS,)), dma((CHIPS,)),
            dma((2,)), dma((2,)),
            dma((CHIPS,)), dma((CHIPS,)),
            dma,
        ],
        compiler_params=pltpu.CompilerParams(
            collective_id=1, has_side_effects=True, vmem_limit_bytes=60 << 20
        ),
    )(payload, key_places, query_places, query_starts)


def doc_starts(doc_lengths):
    return jnp.cumsum(doc_lengths, axis=1) - doc_lengths


def owned_tokens(owner, device, is_image):
    by_block = owner.reshape(BLOCKS, BLOCK)
    mask = by_block == device
    order = np.arange(BLOCK)
    before = jnp.asarray(order[:, None] < order[None, :], jnp.bfloat16)
    rank = jnp.dot(mask.astype(jnp.bfloat16), before, preferred_element_type=jnp.float32)
    tokens = jnp.arange(owner.shape[0], dtype=jnp.int32).reshape(BLOCKS, 1, BLOCK)
    wanted = jnp.arange(6, dtype=jnp.int32).astype(jnp.float32)[None, :, None]
    hit = mask[:, None, :] & (rank[:, None, :] == wanted)
    found = jnp.sum(jnp.where(hit, tokens, 0), axis=2)
    image = found.reshape(ROWS)
    text = jnp.pad(found[:, :2].reshape(TEXT_ROWS), (0, ROWS - TEXT_ROWS))
    return jnp.where(is_image, image, text)


def arrival_codes():
    codes = np.zeros((2, PART), np.int32)
    for core in range(2):
        at = 0
        for chip in range(CHIPS):
            each = 2 if chip < TEXT_CHIPS else 6
            for block in range(8):
                for rank in range(each):
                    codes[core, at] = (block * 64 + 2 * chip + core) * 8 + rank
                    at += 1
    return codes


def arrival_places(owner, seq):
    mine = lax.dynamic_slice_in_dim(owner, seq * SEQ_LEN, SEQ_LEN).reshape(16, BLOCK)
    order = jnp.arange(BLOCK, dtype=jnp.int32)
    same = (mine[:, :, None] == mine[:, None, :]) & (order[None, None, :] < order[None, :, None])
    rank = jnp.sum(same.astype(jnp.int32), axis=2)
    block = jnp.arange(16, dtype=jnp.int32)[:, None] % 8
    code = ((block * 64 + mine) * 8 + rank).reshape(2, SEQ_LEN // 2)
    places = jnp.arange(SEQ_LEN, dtype=jnp.int32).reshape(2, SEQ_LEN // 2)
    hit = code[:, None, None, :] == jnp.asarray(arrival_codes())[None, :, :, None]
    return jnp.sum(jnp.where(hit, places[:, None, None, :], 0), axis=3)


def on_device(stream, norm_gain, qkv_weight, qk_gain, owner, doc_lengths):
    device = lax.axis_index("mod")
    core = device % 2
    seq = device // 2 // HEADS
    is_image = device >= 32
    starts = doc_starts(doc_lengths)

    tokens = owned_tokens(owner, device, is_image)
    absolute = (starts + jnp.arange(SEQS, dtype=jnp.int32)[:, None] * SEQ_LEN).reshape(-1)
    first = jnp.max(jnp.where(absolute[None, :] <= tokens[:, None], absolute[None, :], 0), axis=1)
    half = jnp.arange(HD, dtype=jnp.int32) % (HD // 2)
    freqs = jnp.exp(-math.log(rope_base) * 2.0 * half.astype(jnp.float32) / HD)
    angles = (tokens - first).astype(jnp.float32)[:, None] * freqs[None, :]
    sign = jnp.where(jnp.arange(HD) < HD // 2, -1.0, 1.0).astype(jnp.float32)
    cosines = jnp.cos(angles)
    sines = jnp.sin(angles) * sign[None, :]

    key_places = arrival_places(owner, seq)
    seq_starts = lax.dynamic_slice_in_dim(starts, seq, 1, 0)[0]
    query_places = lax.dynamic_slice_in_dim(key_places, core, 1, 1)[:, 0]
    query_starts = jnp.max(
        jnp.where(seq_starts <= query_places[..., None], seq_starts, 0), axis=-1
    )

    payload = project(
        jnp.transpose(qkv_weight, (0, 2, 1, 3)), stream, norm_gain, cosines, sines, qk_gain
    )
    return attend_all(
        payload, key_places[:, :, None, :], query_places[..., None], query_starts[..., None]
    )


def solution(mesh):
    return jax.shard_map(
        on_device,
        mesh=mesh,
        in_specs=(P("mod", None), P(), P(None, "mod", None, "tp"), P(None, None, "tp"), P(), P()),
        out_specs=P("mod", "tp"),
        check_vma=False,
    )
```

```python
import math

import jax
import jax.numpy as jnp
import numpy as np
from jax import lax
from jax.experimental import pallas as pl
from jax.experimental.pallas import tpu as pltpu
from jax.sharding import PartitionSpec as P

HD = 128
BLOCK = 256
SEQ_LEN = 4096
SEQS = 8
BLOCKS = 128
ROWS = 768
TEXT_ROWS = 256
XS = 4
ZS = 8
CHIPS = XS * ZS
HEADS = 4
WIDTH = HEADS * HD
MODEL = 4096
K_CHUNK = 64
TEXT_CHIPS = CHIPS // 2
TEXT_HALF = 16
IMAGE_HALF = 48
PART = TEXT_CHIPS * (TEXT_HALF + IMAGE_HALF)
Q_TILE = 256
MESH = pl.DeviceIdType.MESH

epsilon = 1e-05
rope_base = 10000.0


def place_of():
    me = lax.axis_index("mod")
    core = lax.rem(me, 2)
    chip = lax.div(me, 2)
    return lax.div(chip, ZS), lax.rem(chip, ZS), core, lax.axis_index("tp")


def project_kernel(
    w_ref, x_ref, gain_ref, cos_ref, sin_ref, qk_ref, out_ref,
    weights, rows, normed, acc,
    z_send, z_recv, x_send, x_recv, s_send, s_recv, c_send, c_recv, load_sem, own_sem,
):
    x, z, core, tp = place_of()
    modality = lax.div(x, 2)
    x_in = x + 1 - 2 * lax.rem(x, 2)
    columns = (x, 3 - x, 3 - x_in)

    def device(xx, zz, cc):
        return ((xx * ZS + zz) * 2 + cc, tp)

    def around(steps):
        return lax.rem(z + steps + 2 * ZS, ZS)

    z_next = (device(x, around(1), core), device(x, around(-1), core))
    partner = device(x_in, z, core)
    across = device(3 - x, z, core)
    sibling = device(x, z, 1 - core)

    def put(src, dst, send, recv, target):
        return pltpu.make_async_remote_copy(
            src_ref=src, dst_ref=dst, send_sem=send, recv_sem=recv,
            device_id=target, device_id_type=MESH,
        )

    def spot(zz, xx):
        return weights.at[zz, :, xx, core]

    def along_z(kind, way, hop, src=None):
        zz = around((1 - hop) if way == 0 else (hop - 1))
        here = spot(zz, columns[kind])
        return put(
            here if src is None else src, here,
            z_send.at[kind, way, hop - 1], z_recv.at[kind, way, hop - 1], z_next[way],
        )

    def to_partner(slot, zz, xx, src=None):
        here = spot(zz, xx)
        return put(here if src is None else src, here, x_send.at[slot], x_recv.at[slot], partner)

    def to_sibling(zz, xx, src=None):
        here = spot(zz, xx)
        return put(
            here if src is None else src, here, s_send.at[zz, xx], s_recv.at[zz, xx], sibling
        )

    def long_way(kind):
        return lax.rem(kind + core, 2)

    barrier = pltpu.get_barrier_semaphore()
    for target in (z_next[0], z_next[1], partner, across, sibling):
        pl.semaphore_signal(barrier, inc=1, device_id=target, device_id_type=MESH)
    pl.semaphore_wait(barrier, 5)

    mine = w_ref.at[modality]
    cross = put(w_ref.at[1 - modality], spot(z, x), c_send, c_recv, across)
    cross.start()
    for way in range(2):
        along_z(0, way, 1, mine).start()
    to_partner(z, z, x, mine).start()
    to_sibling(z, x, mine).start()
    own = pltpu.make_async_copy(mine, spot(z, x), own_sem)
    own.start()
    pieces = [
        pltpu.make_async_copy(
            x_ref.at[pl.ds(i * 128, 128)], rows.at[pl.ds(i * 128, 128)], load_sem.at[i]
        )
        for i in range(ROWS // 128)
    ]
    for piece in pieces:
        piece.start()

    def normalize(i):
        pieces[i].wait()

        @pl.loop(0, 8)
        def _(group):
            at = pl.multiple_of(i * 128 + group * 16, 16)
            sample = rows[pl.ds(at, 16), :].astype(jnp.float32)
            scale = lax.rsqrt(jnp.mean(sample * sample, axis=1, keepdims=True) + epsilon)
            scaled = (sample * scale * gain_ref[pl.ds(modality, 1), :]).astype(jnp.bfloat16)
            for zz in range(ZS):
                for xx in range(XS):
                    k = (xx * ZS + zz) * 128
                    normed[zz, pl.ds(at, 16), xx * 128 : xx * 128 + 128] = scaled[:, k : k + 128]

    normalize(0)
    normalize(1)
    put(w_ref.at[modality], spot(z, 3 - x), c_send, c_recv, across).wait_recv()
    to_partner(ZS, z, 3 - x).start()
    for way in range(2):
        along_z(1, way, 1).start()
    to_sibling(z, 3 - x).start()
    normalize(2)
    normalize(3)
    to_partner(ZS, z, 3 - x_in).wait_recv()
    for way in range(2):
        along_z(2, way, 1).start()
    to_sibling(z, 3 - x_in).start()
    to_partner(z, z, x_in).wait_recv()
    to_sibling(z, x_in).start()
    normalize(4)
    normalize(5)
    own.wait()

    def arrive(kind, way, hop, last):
        zz = around(-hop if way == 0 else hop)
        along_z(kind, way, hop).wait_recv()
        if not last:
            onward = jnp.logical_or(hop < 3, long_way(kind) == way)

            @pl.when(onward)
            def _():
                along_z(kind, way, hop + 1).start()

        if kind == 0:
            to_partner(zz, zz, x).start()
        to_sibling(zz, columns[kind]).start()

    def from_partner(zz):
        to_partner(zz, zz, x_in).wait_recv()
        to_sibling(zz, x_in).start()

    def consume(zz, first=False):
        for xx in range(XS):
            to_sibling(zz, xx).wait_recv()
        lhs = normed[zz]
        for j in range(3):
            part = jnp.dot(
                lhs, weights[zz, j].reshape(XS * 2 * K_CHUNK, WIDTH),
                preferred_element_type=jnp.float32,
            )
            if first:
                acc[j] = part
            else:
                acc[j] += part

    def hop_step(hop, first):
        for kind in range(3):
            for way in range(2):
                arrive(kind, way, hop, False)
        for way in range(2):
            from_partner(around(-hop if way == 0 else hop))
        if first:
            consume(z, True)

    hop_step(1, True)

    @pl.loop(2, 4)
    def _(hop):
        hop_step(hop, False)

        @pl.loop(0, 2)
        def _(way):
            consume(around((hop - 1) * (2 * way - 1)))

    @pl.loop(0, 2)
    def _(way):
        consume(around(3 * (2 * way - 1)))

    far = around(4)
    for kind in range(3):
        for way in range(2):

            @pl.when(long_way(kind) == way)
            def _():
                arrive(kind, way, 4, True)

    from_partner(far)
    consume(far)

    @pl.loop(0, ROWS // 128)
    def _(i):
        at = pl.ds(pl.multiple_of(i * 128, 128), 128)
        cosine = cos_ref[at, :]
        sine = sin_ref[at, :]
        for head in range(HEADS):
            lanes = slice(head * HD, head * HD + HD)
            for j in range(2):
                value = acc[j, at, lanes]
                centred = value - jnp.mean(value, axis=-1, keepdims=True)
                spread = jnp.mean(centred * centred, axis=-1, keepdims=True)
                scaled = centred * lax.rsqrt(spread + epsilon) * qk_ref[modality, pl.ds(j, 1), lanes]
                turned = scaled * cosine + pltpu.roll(scaled, HD // 2, 1) * sine
                out_ref[head, j, at, :] = turned.astype(jnp.bfloat16)
            out_ref[head, 2, at, :] = acc[2, at, lanes].astype(jnp.bfloat16)

    cross.wait_send()
    for kind in range(3):
        for way in range(2):
            for hop in range(1, 4):
                along_z(kind, way, hop).wait_send()

            @pl.when(long_way(kind) == way)
            def _():
                along_z(kind, way, 4).wait_send()

    for slot in range(ZS):
        to_partner(slot, slot, x).wait_send()
    to_partner(ZS, z, x).wait_send()
    for zz in range(ZS):
        for xx in range(XS):
            to_sibling(zz, xx).wait_send()


def project(w, stream, gain, cosines, sines, qk):
    vmem = pl.BlockSpec(memory_space=pltpu.VMEM)
    dma = pltpu.SemaphoreType.DMA
    return pl.pallas_call(
        project_kernel,
        name="gather_project",
        out_shape=jax.ShapeDtypeStruct((HEADS, 3, ROWS, HD), jnp.bfloat16),
        in_specs=[vmem, pl.BlockSpec(memory_space=pl.ANY), vmem, vmem, vmem, vmem],
        out_specs=vmem,
        scratch_shapes=[
            pltpu.VMEM((ZS, 3, XS, 2, K_CHUNK, WIDTH), jnp.bfloat16),
            pltpu.VMEM((ROWS, MODEL), jnp.bfloat16),
            pltpu.VMEM((ZS, ROWS, XS * 128), jnp.bfloat16),
            pltpu.VMEM((3, ROWS, WIDTH), jnp.float32),
            dma((3, 2, 4)), dma((3, 2, 4)),
            dma((ZS + 1,)), dma((ZS + 1,)),
            dma((ZS, XS)), dma((ZS, XS)),
            dma, dma,
            dma((ROWS // 128,)), dma,
        ],
        compiler_params=pltpu.CompilerParams(
            collective_id=0, has_side_effects=True, vmem_limit_bytes=60 << 20
        ),
    )(w, stream, gain, cosines, sines, qk)


def attend_kernel(
    pay_ref, kpos_ref, qpos_ref, qstart_ref, out_ref,
    held, relay, num, den, mixed, blank,
    a_send, a_recv, r_send, r_recv, s_send, s_recv, b_send, b_recv, zero_sem,
):
    x, z, core, tp = place_of()
    me = x * ZS + z
    seq, head = lax.div(me, HEADS), lax.rem(me, HEADS)
    is_image = x >= XS // 2
    sibling = (2 * me + 1 - core, tp)

    def chip(steps):
        return lax.rem(me + steps + CHIPS, CHIPS)

    barrier = pltpu.get_barrier_semaphore()

    @pl.loop(1, CHIPS)
    def _(i):
        pl.semaphore_signal(
            barrier, inc=1, device_id=(2 * chip(i) + core, tp), device_id_type=MESH
        )

    pl.semaphore_signal(barrier, inc=1, device_id=sibling, device_id_type=MESH)
    pl.semaphore_wait(barrier, CHIPS)

    def outbound(to, image, part):
        size = IMAGE_HALF if image else TEXT_HALF
        at = pl.multiple_of((2 * lax.div(to, HEADS) + part) * size, 16)
        return pay_ref.at[lax.rem(to, HEADS), :, pl.ds(at, size)]

    def landing(source, image, part):
        if image:
            at = TEXT_CHIPS * TEXT_HALF + (source - TEXT_CHIPS) * IMAGE_HALF
            size = IMAGE_HALF
        else:
            at = source * TEXT_HALF
            size = TEXT_HALF
        return pl.ds(pl.multiple_of(at, 16), size)

    def send(src, dst, send_sem, recv_sem, to):
        return pltpu.make_async_remote_copy(
            src_ref=src, dst_ref=dst, send_sem=send_sem, recv_sem=recv_sem,
            device_id=(2 * to + core, tp), device_id_type=MESH,
        )

    def both(test, do):
        @pl.when(test)
        def _():
            do(True)

        @pl.when(jnp.logical_not(test))
        def _():
            do(False)

    def start_self(image):
        for part in range(2):
            pltpu.make_async_copy(
                outbound(me, image, part),
                held.at[:, part, core, landing(me, image, part)],
                a_recv.at[me],
            ).start()

    both(is_image, start_self)

    def far_first(i):
        return lax.rem(z + ZS // 2 + lax.div(i, 2) - lax.rem(i, 2) * (1 + 2 * lax.div(i, 2)), ZS)

    @pl.loop(0, ZS - 1)
    def _(i):
        zz = far_first(i)

        def start(image):
            size = IMAGE_HALF if image else TEXT_HALF
            for part in range(2):
                to = x * ZS + zz
                send(
                    outbound(to, image, part), held.at[:, part, core, landing(me, image, part)],
                    a_send.at[0, zz], a_recv.at[me], to,
                ).start()
            for dx in (1, 3, 2):
                to = lax.rem(x + dx, XS) * ZS + z
                rows = pl.ds(
                    pl.multiple_of(
                        2 * lax.div(lax.rem(x + dx, XS) * ZS + zz, HEADS) * size, 16
                    ),
                    2 * size,
                )
                send(
                    pay_ref.at[lax.rem(zz, HEADS), :, rows],
                    relay.at[x, zz, :, pl.ds(0, 2 * size)],
                    a_send.at[dx, zz], r_recv.at[x, zz], to,
                ).start()

        both(is_image, start)

    def start_flat(image):
        for dx in (1, 3, 2):
            to = lax.rem(x + dx, XS) * ZS + z
            for part in range(2):
                send(
                    outbound(to, image, part), held.at[:, part, core, landing(me, image, part)],
                    a_send.at[dx, z], a_recv.at[me], to,
                ).start()

    both(is_image, start_flat)

    @pl.when(jnp.logical_not(is_image))
    def _():
        blank[...] = jnp.zeros_like(blank)
        pltpu.make_async_copy(blank, out_ref.at[pl.ds(TEXT_ROWS, ROWS - TEXT_ROWS)], zero_sem).start()

    def await_rows(image, sem):
        whole = pay_ref.at[0, :, pl.ds(0, 2 * (IMAGE_HALF if image else TEXT_HALF))]
        pltpu.make_async_copy(whole, whole, sem).wait()

    @pl.loop(0, ZS - 1)
    def _(i):
        zz = far_first(i)
        for dx in (1, 3, 2):
            from_x = lax.rem(x + XS - dx, XS)

            def forward(image):
                size = IMAGE_HALF if image else TEXT_HALF
                await_rows(image, r_recv.at[from_x, zz])
                source = from_x * ZS + z
                for part in range(2):
                    send(
                        relay.at[from_x, zz, :, pl.ds(part * size, size)],
                        held.at[:, part, core, landing(source, image, part)],
                        r_send.at[from_x, zz], a_recv.at[source], x * ZS + zz,
                    ).start()

            both(from_x >= XS // 2, forward)

    @pl.loop(0, CHIPS)
    def _(i):
        source = chip(-i)

        def arrive(image):
            size = 2 * (IMAGE_HALF if image else TEXT_HALF)
            whole = pay_ref.at[0, :, pl.ds(0, size)]
            pltpu.make_async_copy(whole, whole, a_recv.at[source]).wait()

        both(source >= TEXT_CHIPS, arrive)

    def share(part):
        mine = held.at[pl.ds(1, 2), part, core]
        return pltpu.make_async_remote_copy(
            src_ref=mine, dst_ref=mine, send_sem=s_send.at[part], recv_sem=s_recv.at[part],
            device_id=sibling, device_id_type=MESH,
        )

    def shared(part):
        other = held.at[pl.ds(1, 2), part, 1 - core]
        return pltpu.make_async_remote_copy(
            src_ref=other, dst_ref=other, send_sem=s_send.at[part], recv_sem=s_recv.at[part],
            device_id=sibling, device_id_type=MESH,
        )

    share(0).start()
    share(1).start()

    def attend(side, first):
        @pl.loop(0, 2 * PART // Q_TILE)
        def _(tile):
            part = lax.div(tile, PART // Q_TILE)
            at = pl.ds(
                pl.multiple_of(lax.rem(tile, PART // Q_TILE) * Q_TILE, Q_TILE), Q_TILE
            )
            query = held[0, part, core, at, :]
            place = qpos_ref[part, at, :]
            start = qstart_ref[part, at, :]

            def step(key_part, fresh):
                keys = held[1, key_part, side]
                values = held[2, key_part, side]
                scores = lax.dot_general(
                    query, keys, (((1,), (1,)), ((), ())), preferred_element_type=jnp.float32
                )
                spots = kpos_ref[key_part, side]
                visible = (spots <= place) & (spots >= start)
                weight = jnp.where(visible, jnp.exp(scores * (1.0 / math.sqrt(HD))), 0.0)
                total = jnp.sum(weight, axis=1, keepdims=True)
                product = jnp.dot(
                    weight.astype(jnp.bfloat16), values, preferred_element_type=jnp.float32
                )
                if fresh:
                    num[part, at, :] = product
                    den[part, at, :] = jnp.broadcast_to(total, product.shape)
                else:
                    num[part, at, :] += product
                    den[part, at, :] += jnp.broadcast_to(total, product.shape)

            step(0, first)

            @pl.when(part == 1)
            def _():
                step(1, False)

    attend(core, True)
    shared(0).wait_recv()
    shared(1).wait_recv()
    attend(1 - core, False)

    @pl.loop(0, 2 * PART // Q_TILE)
    def _(tile):
        part = lax.div(tile, PART // Q_TILE)
        at = pl.ds(pl.multiple_of(lax.rem(tile, PART // Q_TILE) * Q_TILE, Q_TILE), Q_TILE)
        mixed[part, at, :] = (num[part, at, :] / den[part, at, :]).astype(jnp.bfloat16)

    def home(image, part, who_seq, who_head):
        size = IMAGE_HALF if image else TEXT_HALF
        at = pl.multiple_of((2 * who_seq + part) * size, 16)
        return out_ref.at[pl.ds(at, size), pl.ds(pl.multiple_of(who_head * HD, HD), HD)]

    def back(to, image, part):
        return pltpu.make_async_remote_copy(
            src_ref=mixed.at[part, landing(to, image, part)],
            dst_ref=home(image, part, seq, head),
            send_sem=b_send.at[to], recv_sem=b_recv.at[me],
            device_id=(2 * to + core, tp), device_id_type=MESH,
        )

    @pl.loop(1, CHIPS)
    def _(i):
        to = chip(i)

        def start(image):
            for part in range(2):
                back(to, image, part).start()

        both(to >= TEXT_CHIPS, start)

    def back_self(image):
        for part in range(2):
            pltpu.make_async_copy(
                mixed.at[part, landing(me, image, part)],
                home(image, part, seq, head), b_recv.at[me],
            ).start()

    both(is_image, back_self)

    @pl.loop(0, CHIPS)
    def _(i):
        source = chip(-i)

        def arrive(image):
            size = 2 * (IMAGE_HALF if image else TEXT_HALF)
            whole = mixed.at[0, pl.ds(0, size)]
            pltpu.make_async_copy(whole, whole, b_recv.at[source]).wait()

        both(is_image, arrive)

    @pl.loop(1, CHIPS)
    def _(i):
        to = chip(i)

        def returned(image):
            size = 2 * (IMAGE_HALF if image else TEXT_HALF)
            whole = mixed.at[0, pl.ds(0, size)]
            pltpu.make_async_copy(whole, whole, b_send.at[to]).wait()

        both(to >= TEXT_CHIPS, returned)

    share(0).wait_send()
    share(1).wait_send()

    def sent(image):
        @pl.loop(0, ZS)
        def _(zz):
            for dx in range(XS):

                @pl.when(jnp.logical_or(zz != z, dx != 0))
                def _():
                    await_rows(image, a_send.at[dx, zz])

    both(is_image, sent)

    @pl.loop(1, ZS)
    def _(i):
        for dx in range(1, XS):
            from_x = lax.rem(x + dx, XS)

            def relayed(image):
                await_rows(image, r_send.at[from_x, lax.rem(z + i, ZS)])

            both(from_x >= XS // 2, relayed)

    @pl.when(jnp.logical_not(is_image))
    def _():
        pltpu.make_async_copy(blank, out_ref.at[pl.ds(TEXT_ROWS, ROWS - TEXT_ROWS)], zero_sem).wait()


def attend_all(payload, key_places, query_places, query_starts):
    vmem = pl.BlockSpec(memory_space=pltpu.VMEM)
    dma = pltpu.SemaphoreType.DMA
    return pl.pallas_call(
        attend_kernel,
        name="exchange_attend",
        out_shape=jax.ShapeDtypeStruct((ROWS, WIDTH), jnp.bfloat16),
        in_specs=[vmem, vmem, vmem, vmem],
        out_specs=pl.BlockSpec(memory_space=pl.ANY),
        scratch_shapes=[
            pltpu.VMEM((3, 2, 2, PART, HD), jnp.bfloat16),
            pltpu.VMEM((XS, ZS, 3, 2 * IMAGE_HALF, HD), jnp.bfloat16),
            pltpu.VMEM((2, PART, HD), jnp.float32),
            pltpu.VMEM((2, PART, HD), jnp.float32),
            pltpu.VMEM((2, PART, HD), jnp.bfloat16),
            pltpu.VMEM((ROWS - TEXT_ROWS, WIDTH), jnp.bfloat16),
            dma((XS, ZS)), dma((CHIPS,)),
            dma((XS, ZS)), dma((XS, ZS)),
            dma((2,)), dma((2,)),
            dma((CHIPS,)), dma((CHIPS,)),
            dma,
        ],
        compiler_params=pltpu.CompilerParams(
            collective_id=1, has_side_effects=True, vmem_limit_bytes=60 << 20
        ),
    )(payload, key_places, query_places, query_starts)


def doc_starts(doc_lengths):
    return jnp.cumsum(doc_lengths, axis=1) - doc_lengths


def owned_tokens(owner, device, is_image):
    by_block = owner.reshape(BLOCKS, BLOCK)
    mask = by_block == device
    order = np.arange(BLOCK)
    before = jnp.asarray(order[:, None] < order[None, :], jnp.bfloat16)
    rank = jnp.dot(mask.astype(jnp.bfloat16), before, preferred_element_type=jnp.float32)
    tokens = jnp.arange(owner.shape[0], dtype=jnp.int32).reshape(BLOCKS, 1, BLOCK)
    wanted = jnp.arange(6, dtype=jnp.int32).astype(jnp.float32)[None, :, None]
    hit = mask[:, None, :] & (rank[:, None, :] == wanted)
    found = jnp.sum(jnp.where(hit, tokens, 0), axis=2)
    image = found.reshape(ROWS)
    text = jnp.pad(found[:, :2].reshape(TEXT_ROWS), (0, ROWS - TEXT_ROWS))
    return jnp.where(is_image, image, text)


def arrival_codes():
    codes = np.zeros((2, PART), np.int32)
    for core in range(2):
        at = 0
        for chip in range(CHIPS):
            each = 2 if chip < TEXT_CHIPS else 6
            for block in range(8):
                for rank in range(each):
                    codes[core, at] = (block * 64 + 2 * chip + core) * 8 + rank
                    at += 1
    return codes


def arrival_places(owner, seq):
    mine = lax.dynamic_slice_in_dim(owner, seq * SEQ_LEN, SEQ_LEN).reshape(16, BLOCK)
    order = jnp.arange(BLOCK, dtype=jnp.int32)
    same = (mine[:, :, None] == mine[:, None, :]) & (order[None, None, :] < order[None, :, None])
    rank = jnp.sum(same.astype(jnp.int32), axis=2)
    block = jnp.arange(16, dtype=jnp.int32)[:, None] % 8
    code = ((block * 64 + mine) * 8 + rank).reshape(2, SEQ_LEN // 2)
    places = jnp.arange(SEQ_LEN, dtype=jnp.int32).reshape(2, SEQ_LEN // 2)
    hit = code[:, None, None, :] == jnp.asarray(arrival_codes())[None, :, :, None]
    return jnp.sum(jnp.where(hit, places[:, None, None, :], 0), axis=3)


def on_device(stream, norm_gain, qkv_weight, qk_gain, owner, doc_lengths):
    device = lax.axis_index("mod")
    core = device % 2
    seq = device // 2 // HEADS
    is_image = device >= 32
    starts = doc_starts(doc_lengths)

    tokens = owned_tokens(owner, device, is_image)
    absolute = (starts + jnp.arange(SEQS, dtype=jnp.int32)[:, None] * SEQ_LEN).reshape(-1)
    first = jnp.max(jnp.where(absolute[None, :] <= tokens[:, None], absolute[None, :], 0), axis=1)
    half = jnp.arange(HD, dtype=jnp.int32) % (HD // 2)
    freqs = jnp.exp(-math.log(rope_base) * 2.0 * half.astype(jnp.float32) / HD)
    angles = (tokens - first).astype(jnp.float32)[:, None] * freqs[None, :]
    sign = jnp.where(jnp.arange(HD) < HD // 2, -1.0, 1.0).astype(jnp.float32)
    cosines = jnp.cos(angles)
    sines = jnp.sin(angles) * sign[None, :]

    key_places = arrival_places(owner, seq)
    seq_starts = lax.dynamic_slice_in_dim(starts, seq, 1, 0)[0]
    query_places = lax.dynamic_slice_in_dim(key_places, core, 1, 1)[:, 0]
    query_starts = jnp.max(
        jnp.where(seq_starts <= query_places[..., None], seq_starts, 0), axis=-1
    )

    payload = project(
        jnp.transpose(qkv_weight, (0, 2, 1, 3)), stream, norm_gain, cosines, sines, qk_gain
    )
    return attend_all(
        payload, key_places[:, :, None, :], query_places[..., None], query_starts[..., None]
    )


def solution(mesh):
    return jax.shard_map(
        on_device,
        mesh=mesh,
        in_specs=(P("mod", None), P(), P(None, "mod", None, "tp"), P(None, None, "tp"), P(), P()),
        out_specs=P("mod", "tp"),
        check_vma=False,
    )
```

```python
import math

import jax
import jax.numpy as jnp
import numpy as np
from jax import lax
from jax.experimental import pallas as pl
from jax.experimental.pallas import tpu as pltpu
from jax.sharding import PartitionSpec as P

HD = 128
BLOCK = 256
SEQ_LEN = 4096
SEQS = 8
DOCS = 4
BLOCKS = 128
ROWS = 768
TEXT_ROWS = 256
XS = 4
ZS = 8
CHIPS = XS * ZS
HEADS = 4
WIDTH = HEADS * HD
MODEL = 4096
K_CHUNK = 64
TEXT_CHIPS = CHIPS // 2
TEXT_HALF = 16
IMAGE_HALF = 48
PART = TEXT_CHIPS * (TEXT_HALF + IMAGE_HALF)
Q_TILE = 256
MESH = pl.DeviceIdType.MESH

epsilon = 1e-05
rope_base = 10000.0


def place_of():
    me = lax.axis_index("mod")
    core = lax.rem(me, 2)
    chip = lax.div(me, 2)
    return lax.div(chip, ZS), lax.rem(chip, ZS), core, lax.axis_index("tp")


def start_row(lengths_ref):
    lane = lax.broadcasted_iota(jnp.int32, (1, 128), 1)
    row = jnp.full((1, 128), SEQS * SEQ_LEN, jnp.int32)
    for seq in range(SEQS):
        start = jnp.int32(seq * SEQ_LEN)
        for doc in range(DOCS):
            row = jnp.where(lane == seq * DOCS + doc, start, row)
            start = start + lengths_ref[seq, doc]
    return row.astype(jnp.float32)


def start_of(token, starts):
    return jnp.max(jnp.where(starts <= token, starts, 0.0), axis=1, keepdims=True)


def project_kernel(
    lengths_ref, w_ref, x_ref, gain_ref, qk_ref, owner_ref, freq_ref, code_ref, out_ref, places_ref,
    weights, rows, normed, acc, cos_ref, sin_ref, ranked, turned_owner,
    z_send, z_recv, x_send, x_recv, s_send, s_recv, c_send, c_recv, load_sem, own_sem,
):
    x, z, core, tp = place_of()
    modality = lax.div(x, 2)
    x_in = x + 1 - 2 * lax.rem(x, 2)
    columns = (x, 3 - x, 3 - x_in)

    def device(xx, zz, cc):
        return ((xx * ZS + zz) * 2 + cc, tp)

    def around(steps):
        return lax.rem(z + steps + 2 * ZS, ZS)

    z_next = (device(x, around(1), core), device(x, around(-1), core))
    partner = device(x_in, z, core)
    across = device(3 - x, z, core)
    sibling = device(x, z, 1 - core)

    def put(src, dst, send, recv, target):
        return pltpu.make_async_remote_copy(
            src_ref=src, dst_ref=dst, send_sem=send, recv_sem=recv,
            device_id=target, device_id_type=MESH,
        )

    def spot(zz, xx):
        return weights.at[zz, :, xx, core]

    def along_z(kind, way, hop, src=None):
        zz = around((1 - hop) if way == 0 else (hop - 1))
        here = spot(zz, columns[kind])
        return put(
            here if src is None else src, here,
            z_send.at[kind, way, hop - 1], z_recv.at[kind, way, hop - 1], z_next[way],
        )

    def to_partner(slot, zz, xx, src=None):
        here = spot(zz, xx)
        return put(here if src is None else src, here, x_send.at[slot], x_recv.at[slot], partner)

    def to_sibling(zz, xx, src=None):
        here = spot(zz, xx)
        return put(
            here if src is None else src, here, s_send.at[zz, xx], s_recv.at[zz, xx], sibling
        )

    def long_way(kind):
        return lax.rem(kind + core, 2)

    barrier = pltpu.get_barrier_semaphore()
    for target in (z_next[0], z_next[1], partner, across, sibling):
        pl.semaphore_signal(barrier, inc=1, device_id=target, device_id_type=MESH)
    pl.semaphore_wait(barrier, 5)

    mine = w_ref.at[modality]
    cross = put(w_ref.at[1 - modality], spot(z, x), c_send, c_recv, across)
    cross.start()
    for way in range(2):
        along_z(0, way, 1, mine).start()
    to_partner(z, z, x, mine).start()
    to_sibling(z, x, mine).start()
    own = pltpu.make_async_copy(mine, spot(z, x), own_sem)
    own.start()
    pieces = [
        pltpu.make_async_copy(
            x_ref.at[pl.ds(i * 128, 128)], rows.at[pl.ds(i * 128, 128)], load_sem.at[i]
        )
        for i in range(ROWS // 128)
    ]
    for piece in pieces:
        piece.start()

    def normalize(i):
        pieces[i].wait()

        @pl.loop(0, 8)
        def _(group):
            at = pl.multiple_of(i * 128 + group * 16, 16)
            sample = rows[pl.ds(at, 16), :].astype(jnp.float32)
            scale = lax.rsqrt(jnp.mean(sample * sample, axis=1, keepdims=True) + epsilon)
            scaled = (sample * scale * gain_ref[pl.ds(modality, 1), :]).astype(jnp.bfloat16)
            for zz in range(ZS):
                for xx in range(XS):
                    k = (xx * ZS + zz) * 128
                    normed[zz, pl.ds(at, 16), xx * 128 : xx * 128 + 128] = scaled[:, k : k + 128]

    starts = start_row(lengths_ref)
    device_id = (2 * (x * ZS + z) + core).astype(jnp.float32)

    def before(shape, axis):
        down = lax.broadcasted_iota(jnp.int32, shape, 0)
        right = lax.broadcasted_iota(jnp.int32, shape, 1)
        return jnp.where(down < right if axis else right < down, 1.0, 0.0).astype(jnp.bfloat16)

    def rank_owned():
        mine = owner_ref[...].astype(jnp.float32) == device_id
        marks = jnp.where(mine, 1.0, 0.0).astype(jnp.bfloat16)
        rank = jnp.dot(marks, before((BLOCK, BLOCK), 1), preferred_element_type=jnp.float32)
        ranked[...] = jnp.where(mine, rank, 7.0).astype(jnp.bfloat16)

    each = 2 + 4 * modality

    def rope_rows(i):
        row = lax.broadcasted_iota(jnp.int32, (128, BLOCKS), 0) + i * 128
        block = lax.broadcasted_iota(jnp.int32, (128, BLOCKS), 1)
        rank = row - each * block
        here = (rank >= 0) & (rank < each)
        wanted = jnp.sum(jnp.where(here, rank, 0).astype(jnp.float32), axis=1, keepdims=True)
        base = jnp.sum(jnp.where(here, block * BLOCK, 0).astype(jnp.float32), axis=1, keepdims=True)
        spread = jnp.dot(
            jnp.where(here, 1.0, 0.0).astype(jnp.bfloat16), ranked[...],
            preferred_element_type=jnp.float32,
        )
        order = lax.broadcasted_iota(jnp.int32, (128, BLOCK), 1).astype(jnp.float32)
        token = base + jnp.sum(jnp.where(spread == wanted, order, 0.0), axis=1, keepdims=True)
        angle = (token - start_of(token, starts)) * freq_ref[...]
        lane = lax.broadcasted_iota(jnp.int32, (128, HD), 1)
        sine = jnp.sin(angle)
        cos_ref[pl.ds(i * 128, 128), :] = jnp.cos(angle)
        sin_ref[pl.ds(i * 128, 128), :] = jnp.where(lane < HD // 2, -sine, sine)

    def turn_owner():
        down = lax.broadcasted_iota(jnp.int32, (BLOCK, BLOCK), 0)
        right = lax.broadcasted_iota(jnp.int32, (BLOCK, BLOCK), 1)
        turned_owner[...] = lax.dot_general(
            jnp.where(down == right, 1.0, 0.0).astype(jnp.bfloat16),
            owner_ref[...].astype(jnp.float32).astype(jnp.bfloat16),
            (((1,), (1,)), ((), ())), preferred_element_type=jnp.float32,
        ).astype(jnp.bfloat16)

    def arrival_order(part, side):
        first_block = 16 * lax.div(x * ZS + z, HEADS) + 8 * part
        block = code_ref[3:4, :] + first_block.astype(jnp.float32)
        pick = lax.broadcasted_iota(jnp.int32, (BLOCKS, PART), 0).astype(jnp.float32) == block
        owners = jnp.dot(
            turned_owner[...], jnp.where(pick, 1.0, 0.0).astype(jnp.bfloat16),
            preferred_element_type=jnp.float32,
        )
        mine = owners == code_ref[side : side + 1, :]
        rank = jnp.dot(
            before((BLOCK, BLOCK), 0), jnp.where(mine, 1.0, 0.0).astype(jnp.bfloat16),
            preferred_element_type=jnp.float32,
        )
        order = lax.broadcasted_iota(jnp.int32, (BLOCK, PART), 0).astype(jnp.float32)
        hit = mine & (rank == code_ref[2:3, :])
        within = jnp.sum(jnp.where(hit, order, 0.0), axis=0, keepdims=True)
        places_ref[part, side] = within + block * BLOCK

    def arrive(kind, way, hop):
        zz = around(-hop if way == 0 else hop)

        def take():
            along_z(kind, way, hop).wait_recv()
            if hop < 3:
                along_z(kind, way, hop + 1).start()
            if hop == 3:

                @pl.when(long_way(kind) == way)
                def _():
                    along_z(kind, way, 4).start()

            if kind == 0:
                to_partner(zz, zz, x).start()
            to_sibling(zz, columns[kind]).start()

        if hop == 4:
            pl.when(long_way(kind) == way)(take)
        else:
            take()

    def from_partner(zz):
        to_partner(zz, zz, x_in).wait_recv()
        to_sibling(zz, x_in).start()

    def consume(zz, first=False):
        for xx in range(XS):
            to_sibling(zz, xx).wait_recv()

        @pl.loop(0, 3)
        def _(j):
            part = jnp.dot(
                normed[zz], weights[zz, j].reshape(XS * 2 * K_CHUNK, WIDTH),
                preferred_element_type=jnp.float32,
            )
            if first:
                acc[j] = part
            else:
                acc[j] += part

    def consume_two(hop):
        @pl.loop(0, 2)
        def _(way):
            consume(around(hop * (2 * way - 1)))

    normalize(0)
    normalize(1)
    put(mine, spot(z, 3 - x), c_send, c_recv, across).wait_recv()
    to_partner(ZS, z, 3 - x).start()
    for way in range(2):
        along_z(1, way, 1).start()
    to_sibling(z, 3 - x).start()
    arrive(0, 0, 1)
    arrive(0, 1, 1)
    from_partner(z)
    normalize(2)
    normalize(3)
    to_partner(ZS, z, 3 - x_in).wait_recv()
    for way in range(2):
        along_z(2, way, 1).start()
    to_sibling(z, 3 - x_in).start()
    normalize(4)
    normalize(5)

    work = {
        (1, 1): [rank_owned] + [lambda i=i: rope_rows(i) for i in range(2)],
        (1, 0): [lambda i=i: rope_rows(i) for i in range(2, 4)],
        (1, 2): [own.wait, lambda: consume(z, True)],
        (2, 1): [lambda i=i: rope_rows(i) for i in range(4, 6)],
        (2, 0): [turn_owner, lambda: arrival_order(0, 0), lambda: arrival_order(0, 1)],
        (2, 2): [lambda: consume_two(1)],
        (3, 1): [lambda: arrival_order(1, 0), lambda: arrival_order(1, 1)],
        (3, 0): [],
        (3, 2): [lambda: consume_two(2)],
    }
    for hop in range(1, 4):
        for kind in (1, 0, 2):
            for way in range(2):
                arrive(kind, way, hop + 1 if kind == 0 else hop)
            if kind == 2:
                for way in range(2):
                    from_partner(around(-hop if way == 0 else hop))
            for task in work[hop, kind]:
                task()

    far = around(4)
    consume_two(3)
    for kind in (1, 2):
        for way in range(2):
            arrive(kind, way, 4)
    from_partner(far)
    consume(far)

    @pl.loop(0, ROWS // 128)
    def _(i):
        at = pl.ds(pl.multiple_of(i * 128, 128), 128)
        cosine = cos_ref[at, :]
        sine = sin_ref[at, :]
        for head in range(HEADS):
            lanes = slice(head * HD, head * HD + HD)
            for j in range(2):
                value = acc[j, at, lanes]
                centred = value - jnp.mean(value, axis=-1, keepdims=True)
                spread = jnp.mean(centred * centred, axis=-1, keepdims=True)
                scaled = centred * lax.rsqrt(spread + epsilon) * qk_ref[modality, pl.ds(j, 1), lanes]
                turned = scaled * cosine + pltpu.roll(scaled, HD // 2, 1) * sine
                out_ref[head, j, at, :] = turned.astype(jnp.bfloat16)
            out_ref[head, 2, at, :] = acc[2, at, lanes].astype(jnp.bfloat16)

    cross.wait_send()
    for kind in range(3):
        for way in range(2):
            for hop in range(1, 4):
                along_z(kind, way, hop).wait_send()

            @pl.when(long_way(kind) == way)
            def _():
                along_z(kind, way, 4).wait_send()

    for slot in range(ZS):
        to_partner(slot, slot, x).wait_send()
    to_partner(ZS, z, x).wait_send()
    for zz in range(ZS):
        for xx in range(XS):
            to_sibling(zz, xx).wait_send()


def project(lengths, w, stream, gain, qk, owner, freqs, codes):
    vmem = pl.BlockSpec(memory_space=pltpu.VMEM)
    smem = pl.BlockSpec(memory_space=pltpu.SMEM)
    dma = pltpu.SemaphoreType.DMA
    return pl.pallas_call(
        project_kernel,
        name="gather_project",
        out_shape=(
            jax.ShapeDtypeStruct((HEADS, 3, ROWS, HD), jnp.bfloat16),
            jax.ShapeDtypeStruct((2, 2, 1, PART), jnp.float32),
        ),
        in_specs=[smem, vmem, pl.BlockSpec(memory_space=pl.ANY), vmem, vmem, vmem, vmem, vmem],
        out_specs=(vmem, vmem),
        scratch_shapes=[
            pltpu.VMEM((ZS, 3, XS, 2, K_CHUNK, WIDTH), jnp.bfloat16),
            pltpu.VMEM((ROWS, MODEL), jnp.bfloat16),
            pltpu.VMEM((ZS, ROWS, XS * 128), jnp.bfloat16),
            pltpu.VMEM((3, ROWS, WIDTH), jnp.float32),
            pltpu.VMEM((ROWS, HD), jnp.float32),
            pltpu.VMEM((ROWS, HD), jnp.float32),
            pltpu.VMEM((BLOCKS, BLOCK), jnp.bfloat16),
            pltpu.VMEM((BLOCK, BLOCKS), jnp.bfloat16),
            dma((3, 2, 4)), dma((3, 2, 4)),
            dma((ZS + 1,)), dma((ZS + 1,)),
            dma((ZS, XS)), dma((ZS, XS)),
            dma, dma,
            dma((ROWS // 128,)), dma,
        ],
        compiler_params=pltpu.CompilerParams(
            collective_id=0, has_side_effects=True, vmem_limit_bytes=60 << 20
        ),
    )(lengths, w, stream, gain, qk, owner, freqs, codes)


def attend_kernel(
    lengths_ref, pay_ref, kpos_ref, out_ref,
    held, relay, qpos_ref, qstart_ref, num, den, mixed, blank,
    a_send, a_recv, r_send, r_recv, s_send, s_recv, b_send, b_recv, zero_sem,
):
    x, z, core, tp = place_of()
    me = x * ZS + z
    seq, head = lax.div(me, HEADS), lax.rem(me, HEADS)
    is_image = x >= XS // 2
    sibling = (2 * me + 1 - core, tp)

    def chip(steps):
        return lax.rem(me + steps + CHIPS, CHIPS)

    barrier = pltpu.get_barrier_semaphore()

    @pl.loop(1, CHIPS)
    def _(i):
        pl.semaphore_signal(
            barrier, inc=1, device_id=(2 * chip(i) + core, tp), device_id_type=MESH
        )

    pl.semaphore_signal(barrier, inc=1, device_id=sibling, device_id_type=MESH)
    pl.semaphore_wait(barrier, CHIPS)

    def outbound(to, image, part):
        size = IMAGE_HALF if image else TEXT_HALF
        at = pl.multiple_of((2 * lax.div(to, HEADS) + part) * size, 16)
        return pay_ref.at[lax.rem(to, HEADS), :, pl.ds(at, size)]

    def landing(source, image, part):
        if image:
            at = TEXT_CHIPS * TEXT_HALF + (source - TEXT_CHIPS) * IMAGE_HALF
            size = IMAGE_HALF
        else:
            at = source * TEXT_HALF
            size = TEXT_HALF
        return pl.ds(pl.multiple_of(at, 16), size)

    def send(src, dst, send_sem, recv_sem, to):
        return pltpu.make_async_remote_copy(
            src_ref=src, dst_ref=dst, send_sem=send_sem, recv_sem=recv_sem,
            device_id=(2 * to + core, tp), device_id_type=MESH,
        )

    def both(test, do):
        @pl.when(test)
        def _():
            do(True)

        @pl.when(jnp.logical_not(test))
        def _():
            do(False)

    def start_self(image):
        for part in range(2):
            pltpu.make_async_copy(
                outbound(me, image, part),
                held.at[:, part, core, landing(me, image, part)],
                a_recv.at[me],
            ).start()

    both(is_image, start_self)

    def far_first(i):
        return lax.rem(z + ZS // 2 + lax.div(i, 2) - lax.rem(i, 2) * (1 + 2 * lax.div(i, 2)), ZS)

    @pl.loop(0, ZS - 1)
    def _(i):
        zz = far_first(i)

        def start(image):
            size = IMAGE_HALF if image else TEXT_HALF
            for part in range(2):
                to = x * ZS + zz
                send(
                    outbound(to, image, part), held.at[:, part, core, landing(me, image, part)],
                    a_send.at[0, zz], a_recv.at[me], to,
                ).start()
            for dx in (1, 3, 2):
                to = lax.rem(x + dx, XS) * ZS + z
                rows = pl.ds(
                    pl.multiple_of(
                        2 * lax.div(lax.rem(x + dx, XS) * ZS + zz, HEADS) * size, 16
                    ),
                    2 * size,
                )
                send(
                    pay_ref.at[lax.rem(zz, HEADS), :, rows],
                    relay.at[x, zz, :, pl.ds(0, 2 * size)],
                    a_send.at[dx, zz], r_recv.at[x, zz], to,
                ).start()

        both(is_image, start)

    def start_flat(image):
        for dx in (1, 3, 2):
            to = lax.rem(x + dx, XS) * ZS + z
            for part in range(2):
                send(
                    outbound(to, image, part), held.at[:, part, core, landing(me, image, part)],
                    a_send.at[dx, z], a_recv.at[me], to,
                ).start()

    both(is_image, start_flat)

    @pl.when(jnp.logical_not(is_image))
    def _():
        blank[...] = jnp.zeros_like(blank)
        pltpu.make_async_copy(blank, out_ref.at[pl.ds(TEXT_ROWS, ROWS - TEXT_ROWS)], zero_sem).start()

    starts = start_row(lengths_ref)

    @pl.loop(0, 2)
    def _(part):
        down = lax.broadcasted_iota(jnp.int32, (128, 128), 0)
        right = lax.broadcasted_iota(jnp.int32, (128, 128), 1)
        row = kpos_ref[part, core]
        for k in range(PART // 128):
            at = slice(k * 128, k * 128 + 128)
            token = jnp.sum(jnp.where(down == right, row[:, at], 0.0), axis=1, keepdims=True)
            qpos_ref[part, at, :] = token
            qstart_ref[part, at, :] = start_of(token, starts)

    def await_rows(image, sem):
        whole = pay_ref.at[0, :, pl.ds(0, 2 * (IMAGE_HALF if image else TEXT_HALF))]
        pltpu.make_async_copy(whole, whole, sem).wait()

    @pl.loop(0, ZS - 1)
    def _(i):
        zz = far_first(i)
        for dx in (1, 3, 2):
            from_x = lax.rem(x + XS - dx, XS)

            def forward(image):
                size = IMAGE_HALF if image else TEXT_HALF
                await_rows(image, r_recv.at[from_x, zz])
                source = from_x * ZS + z
                for part in range(2):
                    send(
                        relay.at[from_x, zz, :, pl.ds(part * size, size)],
                        held.at[:, part, core, landing(source, image, part)],
                        r_send.at[from_x, zz], a_recv.at[source], x * ZS + zz,
                    ).start()

            both(from_x >= XS // 2, forward)

    @pl.loop(0, CHIPS)
    def _(i):
        source = chip(-i)

        def arrive(image):
            size = 2 * (IMAGE_HALF if image else TEXT_HALF)
            whole = pay_ref.at[0, :, pl.ds(0, size)]
            pltpu.make_async_copy(whole, whole, a_recv.at[source]).wait()

        both(source >= TEXT_CHIPS, arrive)

    def share(part):
        mine = held.at[pl.ds(1, 2), part, core]
        return pltpu.make_async_remote_copy(
            src_ref=mine, dst_ref=mine, send_sem=s_send.at[part], recv_sem=s_recv.at[part],
            device_id=sibling, device_id_type=MESH,
        )

    def shared(part):
        other = held.at[pl.ds(1, 2), part, 1 - core]
        return pltpu.make_async_remote_copy(
            src_ref=other, dst_ref=other, send_sem=s_send.at[part], recv_sem=s_recv.at[part],
            device_id=sibling, device_id_type=MESH,
        )

    share(0).start()
    share(1).start()

    def attend(side, first):
        @pl.loop(0, 2 * PART // Q_TILE)
        def _(tile):
            part = lax.div(tile, PART // Q_TILE)
            at = pl.ds(
                pl.multiple_of(lax.rem(tile, PART // Q_TILE) * Q_TILE, Q_TILE), Q_TILE
            )
            query = held[0, part, core, at, :]
            place = qpos_ref[part, at, :]
            start = qstart_ref[part, at, :]

            def step(key_part, fresh):
                keys = held[1, key_part, side]
                values = held[2, key_part, side]
                scores = lax.dot_general(
                    query, keys, (((1,), (1,)), ((), ())), preferred_element_type=jnp.float32
                )
                spots = kpos_ref[key_part, side]
                visible = (spots <= place) & (spots >= start)
                weight = jnp.where(visible, jnp.exp(scores * (1.0 / math.sqrt(HD))), 0.0)
                total = jnp.sum(weight, axis=1, keepdims=True)
                product = jnp.dot(
                    weight.astype(jnp.bfloat16), values, preferred_element_type=jnp.float32
                )
                if fresh:
                    num[part, at, :] = product
                    den[part, at, :] = jnp.broadcast_to(total, product.shape)
                else:
                    num[part, at, :] += product
                    den[part, at, :] += jnp.broadcast_to(total, product.shape)

            step(0, first)

            @pl.when(part == 1)
            def _():
                step(1, False)

    attend(core, True)
    shared(0).wait_recv()
    shared(1).wait_recv()
    attend(1 - core, False)

    @pl.loop(0, 2 * PART // Q_TILE)
    def _(tile):
        part = lax.div(tile, PART // Q_TILE)
        at = pl.ds(pl.multiple_of(lax.rem(tile, PART // Q_TILE) * Q_TILE, Q_TILE), Q_TILE)
        mixed[part, at, :] = (num[part, at, :] / den[part, at, :]).astype(jnp.bfloat16)

    def home(image, part, who_seq, who_head):
        size = IMAGE_HALF if image else TEXT_HALF
        at = pl.multiple_of((2 * who_seq + part) * size, 16)
        return out_ref.at[pl.ds(at, size), pl.ds(pl.multiple_of(who_head * HD, HD), HD)]

    def back(to, image, part):
        return pltpu.make_async_remote_copy(
            src_ref=mixed.at[part, landing(to, image, part)],
            dst_ref=home(image, part, seq, head),
            send_sem=b_send.at[to], recv_sem=b_recv.at[me],
            device_id=(2 * to + core, tp), device_id_type=MESH,
        )

    @pl.loop(1, CHIPS)
    def _(i):
        to = chip(i)

        def start(image):
            for part in range(2):
                back(to, image, part).start()

        both(to >= TEXT_CHIPS, start)

    def back_self(image):
        for part in range(2):
            pltpu.make_async_copy(
                mixed.at[part, landing(me, image, part)],
                home(image, part, seq, head), b_recv.at[me],
            ).start()

    both(is_image, back_self)

    @pl.loop(0, CHIPS)
    def _(i):
        source = chip(-i)

        def arrive(image):
            size = 2 * (IMAGE_HALF if image else TEXT_HALF)
            whole = mixed.at[0, pl.ds(0, size)]
            pltpu.make_async_copy(whole, whole, b_recv.at[source]).wait()

        both(is_image, arrive)

    @pl.loop(1, CHIPS)
    def _(i):
        to = chip(i)

        def returned(image):
            size = 2 * (IMAGE_HALF if image else TEXT_HALF)
            whole = mixed.at[0, pl.ds(0, size)]
            pltpu.make_async_copy(whole, whole, b_send.at[to]).wait()

        both(to >= TEXT_CHIPS, returned)

    share(0).wait_send()
    share(1).wait_send()

    def sent(image):
        @pl.loop(0, ZS)
        def _(zz):
            for dx in range(XS):

                @pl.when(jnp.logical_or(zz != z, dx != 0))
                def _():
                    await_rows(image, a_send.at[dx, zz])

    both(is_image, sent)

    @pl.loop(1, ZS)
    def _(i):
        for dx in range(1, XS):
            from_x = lax.rem(x + dx, XS)

            def relayed(image):
                await_rows(image, r_send.at[from_x, lax.rem(z + i, ZS)])

            both(from_x >= XS // 2, relayed)

    @pl.when(jnp.logical_not(is_image))
    def _():
        pltpu.make_async_copy(blank, out_ref.at[pl.ds(TEXT_ROWS, ROWS - TEXT_ROWS)], zero_sem).wait()


def attend_all(lengths, payload, places):
    vmem = pl.BlockSpec(memory_space=pltpu.VMEM)
    dma = pltpu.SemaphoreType.DMA
    return pl.pallas_call(
        attend_kernel,
        name="exchange_attend",
        out_shape=jax.ShapeDtypeStruct((ROWS, WIDTH), jnp.bfloat16),
        in_specs=[pl.BlockSpec(memory_space=pltpu.SMEM), vmem, vmem],
        out_specs=pl.BlockSpec(memory_space=pl.ANY),
        scratch_shapes=[
            pltpu.VMEM((3, 2, 2, PART, HD), jnp.bfloat16),
            pltpu.VMEM((XS, ZS, 3, 2 * IMAGE_HALF, HD), jnp.bfloat16),
            pltpu.VMEM((2, PART, 1), jnp.float32),
            pltpu.VMEM((2, PART, 1), jnp.float32),
            pltpu.VMEM((2, PART, HD), jnp.float32),
            pltpu.VMEM((2, PART, HD), jnp.float32),
            pltpu.VMEM((2, PART, HD), jnp.bfloat16),
            pltpu.VMEM((ROWS - TEXT_ROWS, WIDTH), jnp.bfloat16),
            dma((XS, ZS)), dma((CHIPS,)),
            dma((XS, ZS)), dma((XS, ZS)),
            dma((2,)), dma((2,)),
            dma((CHIPS,)), dma((CHIPS,)),
            dma,
        ],
        compiler_params=pltpu.CompilerParams(
            collective_id=1, has_side_effects=True, vmem_limit_bytes=60 << 20
        ),
    )(lengths, payload, places)


def arrival_codes():
    codes = np.zeros((8, PART), np.float32)
    at = 0
    for chip in range(CHIPS):
        each = 2 if chip < TEXT_CHIPS else 6
        for block in range(8):
            for rank in range(each):
                codes[:4, at] = (2 * chip, 2 * chip + 1, rank, block)
                at += 1
    return codes


def on_device(stream, norm_gain, qkv_weight, qk_gain, owner, doc_lengths):
    half = np.arange(HD) % (HD // 2)
    freqs = np.exp(-math.log(rope_base) * 2.0 * half / HD).astype(np.float32)[None, :]
    payload, places = project(
        doc_lengths, jnp.transpose(qkv_weight, (0, 2, 1, 3)), stream, norm_gain, qk_gain,
        owner.reshape(BLOCKS, BLOCK), jnp.asarray(freqs), jnp.asarray(arrival_codes()),
    )
    return attend_all(doc_lengths, payload, places)


def solution(mesh):
    return jax.shard_map(
        on_device,
        mesh=mesh,
        in_specs=(P("mod", None), P(), P(None, "mod", None, "tp"), P(None, None, "tp"), P(), P()),
        out_specs=P("mod", "tp"),
        check_vma=False,
    )
```

```python
import math

import jax
import jax.numpy as jnp
import numpy as np
from jax import lax
from jax.experimental import pallas as pl
from jax.experimental.pallas import tpu as pltpu
from jax.sharding import PartitionSpec as P

HD = 128
BLOCK = 256
SEQ_LEN = 4096
SEQS = 8
DOCS = 4
BLOCKS = 128
ROWS = 768
TEXT_ROWS = 256
XS = 4
ZS = 8
CHIPS = XS * ZS
HEADS = 4
WIDTH = HEADS * HD
MODEL = 4096
K_CHUNK = 64
TEXT_CHIPS = CHIPS // 2
TEXT_HALF = 16
IMAGE_HALF = 48
PART = TEXT_CHIPS * (TEXT_HALF + IMAGE_HALF)
Q_TILE = 256
MESH = pl.DeviceIdType.MESH
GROUPS = (pl.ds(0, 2), pl.ds(2, 1))

epsilon = 1e-05
rope_base = 10000.0


def place_of():
    me = lax.axis_index("mod")
    core = lax.rem(me, 2)
    chip = lax.div(me, 2)
    return lax.div(chip, ZS), lax.rem(chip, ZS), core, lax.axis_index("tp")


def start_row(lengths_ref):
    lane = lax.broadcasted_iota(jnp.int32, (1, 128), 1)
    row = jnp.full((1, 128), SEQS * SEQ_LEN, jnp.int32)
    for seq in range(SEQS):
        start = jnp.int32(seq * SEQ_LEN)
        for doc in range(DOCS):
            row = jnp.where(lane == seq * DOCS + doc, start, row)
            start = start + lengths_ref[doc, seq]
    return row.astype(jnp.float32)


def start_of(token, starts):
    return jnp.max(jnp.where(starts <= token, starts, 0.0), axis=1, keepdims=True)


def project_kernel(
    lengths_ref, w_ref, x_ref, gain_ref, qk_ref, owner_ref, freq_ref, code_ref, out_ref, places_ref,
    weights, rows, normed, acc, cos_ref, sin_ref, blocked, ranked, turned_owner,
    z_send, z_recv, x_send, x_recv, s_send, s_recv, c_send, c_recv, load_sem, own_sem,
):
    x, z, core, tp = place_of()
    modality = lax.div(x, 2)
    x_in = x + 1 - 2 * lax.rem(x, 2)
    columns = (x, 3 - x, 3 - x_in)

    def device(xx, zz, cc):
        return ((xx * ZS + zz) * 2 + cc, tp)

    def around(steps):
        return lax.rem(z + steps + 2 * ZS, ZS)

    z_next = (device(x, around(1), core), device(x, around(-1), core))
    partner = device(x_in, z, core)
    across = device(3 - x, z, core)
    sibling = device(x, z, 1 - core)

    def put(src, dst, send, recv, target):
        return pltpu.make_async_remote_copy(
            src_ref=src, dst_ref=dst, send_sem=send, recv_sem=recv,
            device_id=target, device_id_type=MESH,
        )

    def spot(group, zz, xx):
        return weights.at[zz, GROUPS[group], xx, core]

    def mine(group):
        return w_ref.at[modality, GROUPS[group]]

    def along_z(group, kind, way, hop, src=None):
        zz = around((1 - hop) if way == 0 else (hop - 1))
        here = spot(group, zz, columns[kind])
        at = (group, kind, way, hop - 1)
        return put(
            here if src is None else src, here, z_send.at[at], z_recv.at[at], z_next[way]
        )

    def to_partner(group, slot, zz, xx, src=None):
        here = spot(group, zz, xx)
        return put(
            here if src is None else src, here,
            x_send.at[group, slot], x_recv.at[group, slot], partner,
        )

    def to_sibling(group, zz, xx, src=None):
        here = spot(group, zz, xx)
        return put(
            here if src is None else src, here,
            s_send.at[group, zz, xx], s_recv.at[group, zz, xx], sibling,
        )

    def cross(group):
        return put(
            w_ref.at[1 - modality, GROUPS[group]], spot(group, z, x),
            c_send.at[group], c_recv.at[group], across,
        )

    def long_way(kind):
        return lax.rem(kind + core, 2)

    barrier = pltpu.get_barrier_semaphore()
    for target in (z_next[0], z_next[1], partner, across, sibling):
        pl.semaphore_signal(barrier, inc=1, device_id=target, device_id_type=MESH)
    pl.semaphore_wait(barrier, 5)

    cross(0).start()
    for way in range(2):
        along_z(0, 0, way, 1, mine(0)).start()
    to_partner(0, z, z, x, mine(0)).start()
    to_sibling(0, z, x, mine(0)).start()
    cross(1).start()
    own = pltpu.make_async_copy(w_ref.at[modality], weights.at[z, :, x, core], own_sem)
    own.start()
    pieces = [
        pltpu.make_async_copy(
            x_ref.at[pl.ds(i * 128, 128)], rows.at[pl.ds(i * 128, 128)], load_sem.at[i]
        )
        for i in range(ROWS // 128)
    ]
    for piece in pieces:
        piece.start()

    def normalize(i):
        pieces[i].wait()

        @pl.loop(0, 8)
        def _(group):
            at = pl.multiple_of(i * 128 + group * 16, 16)
            sample = rows[pl.ds(at, 16), :].astype(jnp.float32)
            scale = lax.rsqrt(jnp.mean(sample * sample, axis=1, keepdims=True) + epsilon)
            scaled = (sample * scale * gain_ref[pl.ds(modality, 1), :]).astype(jnp.bfloat16)
            for zz in range(ZS):
                for xx in range(XS):
                    k = (xx * ZS + zz) * 128
                    normed[zz, pl.ds(at, 16), xx * 128 : xx * 128 + 128] = scaled[:, k : k + 128]

    starts = start_row(lengths_ref)
    device_id = (2 * (x * ZS + z) + core).astype(jnp.float32)

    def before(shape, axis):
        down = lax.broadcasted_iota(jnp.int32, shape, 0)
        right = lax.broadcasted_iota(jnp.int32, shape, 1)
        return jnp.where(down < right if axis else right < down, 1.0, 0.0).astype(jnp.bfloat16)

    def by_block():
        row = lax.broadcasted_iota(jnp.int32, (BLOCKS, 2 * BLOCKS), 0)
        column = lax.broadcasted_iota(jnp.int32, (BLOCKS, 2 * BLOCKS), 1)
        flat = owner_ref[...].astype(jnp.float32).astype(jnp.bfloat16)
        for side in range(2):
            pick = jnp.where(column == 2 * row + side, 1.0, 0.0).astype(jnp.bfloat16)
            blocked[:, side * 128 : side * 128 + 128] = jnp.dot(
                pick, flat, preferred_element_type=jnp.float32
            )

    def rank_owned():
        owned = blocked[...] == device_id
        marks = jnp.where(owned, 1.0, 0.0).astype(jnp.bfloat16)
        rank = jnp.dot(marks, before((BLOCK, BLOCK), 1), preferred_element_type=jnp.float32)
        ranked[...] = jnp.where(owned, rank, 7.0).astype(jnp.bfloat16)

    each = 2 + 4 * modality

    def rope_rows(i):
        row = lax.broadcasted_iota(jnp.int32, (128, BLOCKS), 0) + i * 128
        block = lax.broadcasted_iota(jnp.int32, (128, BLOCKS), 1)
        rank = row - each * block
        here = (rank >= 0) & (rank < each)
        wanted = jnp.sum(jnp.where(here, rank, 0).astype(jnp.float32), axis=1, keepdims=True)
        base = jnp.sum(jnp.where(here, block * BLOCK, 0).astype(jnp.float32), axis=1, keepdims=True)
        spread = jnp.dot(
            jnp.where(here, 1.0, 0.0).astype(jnp.bfloat16), ranked[...],
            preferred_element_type=jnp.float32,
        )
        order = lax.broadcasted_iota(jnp.int32, (128, BLOCK), 1).astype(jnp.float32)
        token = base + jnp.sum(jnp.where(spread == wanted, order, 0.0), axis=1, keepdims=True)
        angle = (token - start_of(token, starts)) * freq_ref[...]
        lane = lax.broadcasted_iota(jnp.int32, (128, HD), 1)
        sine = jnp.sin(angle)
        cos_ref[pl.ds(i * 128, 128), :] = jnp.cos(angle)
        sin_ref[pl.ds(i * 128, 128), :] = jnp.where(lane < HD // 2, -sine, sine)

    def turn_owner():
        down = lax.broadcasted_iota(jnp.int32, (BLOCK, BLOCK), 0)
        right = lax.broadcasted_iota(jnp.int32, (BLOCK, BLOCK), 1)
        turned_owner[...] = lax.dot_general(
            jnp.where(down == right, 1.0, 0.0).astype(jnp.bfloat16),
            blocked[...].astype(jnp.bfloat16),
            (((1,), (1,)), ((), ())), preferred_element_type=jnp.float32,
        ).astype(jnp.bfloat16)

    def arrival_order(part, side):
        first_block = 16 * lax.div(x * ZS + z, HEADS) + 8 * part
        block = code_ref[3:4, :] + first_block.astype(jnp.float32)
        pick = lax.broadcasted_iota(jnp.int32, (BLOCKS, PART), 0).astype(jnp.float32) == block
        owners = jnp.dot(
            turned_owner[...], jnp.where(pick, 1.0, 0.0).astype(jnp.bfloat16),
            preferred_element_type=jnp.float32,
        )
        same = owners == code_ref[side : side + 1, :]
        rank = jnp.dot(
            before((BLOCK, BLOCK), 0), jnp.where(same, 1.0, 0.0).astype(jnp.bfloat16),
            preferred_element_type=jnp.float32,
        )
        order = lax.broadcasted_iota(jnp.int32, (BLOCK, PART), 0).astype(jnp.float32)
        hit = same & (rank == code_ref[2:3, :])
        within = jnp.sum(jnp.where(hit, order, 0.0), axis=0, keepdims=True)
        places_ref[part, side] = within + block * BLOCK

    def arrive(group, kind, way, hop):
        zz = around(-hop if way == 0 else hop)

        def take():
            along_z(group, kind, way, hop).wait_recv()
            if hop < 3:
                along_z(group, kind, way, hop + 1).start()
            if hop == 3:

                @pl.when(long_way(kind) == way)
                def _():
                    along_z(group, kind, way, 4).start()

            if kind == 0:
                to_partner(group, zz, zz, x).start()
            to_sibling(group, zz, columns[kind]).start()

        if hop == 4:
            pl.when(long_way(kind) == way)(take)
        else:
            take()

    def from_partner(group, zz):
        to_partner(group, zz, zz, x_in).wait_recv()
        to_sibling(group, zz, x_in).start()

    def take_cross(group):
        put(
            mine(group), spot(group, z, 3 - x), c_send.at[group], c_recv.at[group], across
        ).wait_recv()
        to_partner(group, ZS, z, 3 - x).start()

    def consume(group, zz, first=False):
        for xx in range(XS):
            to_sibling(group, zz, xx).wait_recv()

        @pl.loop(GROUPS[group].start, GROUPS[group].start + GROUPS[group].size)
        def _(j):
            part = jnp.dot(
                normed[zz], weights[zz, j].reshape(XS * 2 * K_CHUNK, WIDTH),
                preferred_element_type=jnp.float32,
            )
            if first:
                acc[j] = part
            else:
                acc[j] += part

    def consume_two(group, hop):
        @pl.loop(0, 2)
        def _(way):
            consume(group, around(hop * (2 * way - 1)))

    def finish_rows(i):
        at = pl.ds(i * 128, 128)
        cosine = cos_ref[at, :]
        sine = sin_ref[at, :]
        for head in range(HEADS):
            lanes = slice(head * HD, head * HD + HD)
            for j in range(2):
                value = acc[j, at, lanes]
                centred = value - jnp.mean(value, axis=-1, keepdims=True)
                spread = jnp.mean(centred * centred, axis=-1, keepdims=True)
                scaled = centred * lax.rsqrt(spread + epsilon) * qk_ref[modality, pl.ds(j, 1), lanes]
                turned = scaled * cosine + pltpu.roll(scaled, HD // 2, 1) * sine
                out_ref[head, j, at, :] = turned.astype(jnp.bfloat16)

    normalize(0)
    normalize(1)
    take_cross(0)
    for way in range(2):
        along_z(0, 1, way, 1).start()
    to_sibling(0, z, 3 - x).start()
    arrive(0, 0, 0, 1)
    arrive(0, 0, 1, 1)
    from_partner(0, z)
    normalize(2)
    normalize(3)
    to_partner(0, ZS, z, 3 - x_in).wait_recv()
    for way in range(2):
        along_z(0, 2, way, 1).start()
    to_sibling(0, z, 3 - x_in).start()
    normalize(4)
    normalize(5)

    def start_values():
        take_cross(1)
        to_partner(1, z, z, x, mine(1)).start()

    def send_values():
        to_partner(1, ZS, z, 3 - x_in).wait_recv()
        for way in range(2):
            along_z(1, 0, way, 1, mine(1)).start()
        for way in range(2):
            along_z(1, 1, way, 1).start()
        for way in range(2):
            along_z(1, 2, way, 1).start()
        to_sibling(1, z, x, mine(1)).start()
        to_sibling(1, z, 3 - x).start()
        to_sibling(1, z, 3 - x_in).start()
        from_partner(1, z)

    def hops(group, work):
        for hop in range(1, 4):
            for kind in (1, 0, 2):
                for way in range(2):
                    arrive(group, kind, way, hop + 1 if kind == 0 else hop)
                if kind == 2:
                    for way in range(2):
                        from_partner(group, around(-hop if way == 0 else hop))
                for task in work[hop, kind]:
                    task()

    far = around(4)

    def last_hop(group):
        for kind in (1, 2):
            for way in range(2):
                arrive(group, kind, way, 4)
        from_partner(group, far)

    hops(0, {
        (1, 1): [by_block, rank_owned] + [lambda i=i: rope_rows(i) for i in range(2)],
        (1, 0): [lambda i=i: rope_rows(i) for i in range(2, 4)],
        (1, 2): [start_values, own.wait, lambda: consume(0, z, True)],
        (2, 1): [lambda i=i: rope_rows(i) for i in range(4, 6)],
        (2, 0): [turn_owner, lambda: arrival_order(0, 0), lambda: arrival_order(0, 1)],
        (2, 2): [send_values, lambda: consume_two(0, 1)],
        (3, 1): [lambda: arrival_order(1, 0), lambda: arrival_order(1, 1)],
        (3, 0): [],
        (3, 2): [lambda: consume_two(0, 2)],
    })
    arrive(1, 0, 0, 1)
    arrive(1, 0, 1, 1)
    last_hop(0)
    consume_two(0, 3)
    finish = [lambda i=i: finish_rows(i) for i in range(ROWS // 128)]
    hops(1, {
        (1, 1): [lambda: consume(0, far)],
        (1, 0): finish[0:1],
        (1, 2): finish[1:2],
        (2, 1): finish[2:3],
        (2, 0): finish[3:4],
        (2, 2): finish[4:5],
        (3, 1): finish[5:6],
        (3, 0): [lambda: consume(1, z, True)],
        (3, 2): [lambda: consume_two(1, 1), lambda: consume_two(1, 2)],
    })
    last_hop(1)
    consume_two(1, 3)
    consume(1, far)

    @pl.loop(0, ROWS // 128)
    def _(i):
        at = pl.ds(pl.multiple_of(i * 128, 128), 128)
        for head in range(HEADS):
            out_ref[head, 2, at, :] = acc[2, at, head * HD : head * HD + HD].astype(jnp.bfloat16)

    for group in range(2):
        cross(group).wait_send()
        for kind in range(3):
            for way in range(2):
                for hop in range(1, 4):
                    along_z(group, kind, way, hop).wait_send()

                @pl.when(long_way(kind) == way)
                def _():
                    along_z(group, kind, way, 4).wait_send()

        for slot in range(ZS):
            to_partner(group, slot, slot, x).wait_send()
        to_partner(group, ZS, z, x).wait_send()
        for zz in range(ZS):
            for xx in range(XS):
                to_sibling(group, zz, xx).wait_send()


def project(lengths, w, stream, gain, qk, owner, freqs, codes):
    vmem = pl.BlockSpec(memory_space=pltpu.VMEM)
    smem = pl.BlockSpec(memory_space=pltpu.SMEM)
    dma = pltpu.SemaphoreType.DMA
    return pl.pallas_call(
        project_kernel,
        name="gather_project",
        out_shape=(
            jax.ShapeDtypeStruct((HEADS, 3, ROWS, HD), jnp.bfloat16),
            jax.ShapeDtypeStruct((2, 2, 1, PART), jnp.float32),
        ),
        in_specs=[smem, vmem, pl.BlockSpec(memory_space=pl.ANY), vmem, vmem, vmem, vmem, vmem],
        out_specs=(vmem, vmem),
        scratch_shapes=[
            pltpu.VMEM((ZS, 3, XS, 2, K_CHUNK, WIDTH), jnp.bfloat16),
            pltpu.VMEM((ROWS, MODEL), jnp.bfloat16),
            pltpu.VMEM((ZS, ROWS, XS * 128), jnp.bfloat16),
            pltpu.VMEM((3, ROWS, WIDTH), jnp.float32),
            pltpu.VMEM((ROWS, HD), jnp.float32),
            pltpu.VMEM((ROWS, HD), jnp.float32),
            pltpu.VMEM((BLOCKS, BLOCK), jnp.float32),
            pltpu.VMEM((BLOCKS, BLOCK), jnp.bfloat16),
            pltpu.VMEM((BLOCK, BLOCKS), jnp.bfloat16),
            dma((2, 3, 2, 4)), dma((2, 3, 2, 4)),
            dma((2, ZS + 1)), dma((2, ZS + 1)),
            dma((2, ZS, XS)), dma((2, ZS, XS)),
            dma((2,)), dma((2,)),
            dma((ROWS // 128,)), dma,
        ],
        compiler_params=pltpu.CompilerParams(
            collective_id=0, has_side_effects=True, vmem_limit_bytes=60 << 20
        ),
    )(lengths, w, stream, gain, qk, owner, freqs, codes)


def attend_kernel(
    lengths_ref, pay_ref, kpos_ref, out_ref,
    held, relay, qpos_ref, qstart_ref, num, den, mixed, blank,
    a_send, a_recv, r_send, r_recv, s_send, s_recv, b_send, b_recv, zero_sem,
):
    x, z, core, tp = place_of()
    me = x * ZS + z
    seq, head = lax.div(me, HEADS), lax.rem(me, HEADS)
    is_image = x >= XS // 2
    sibling = (2 * me + 1 - core, tp)

    def chip(steps):
        return lax.rem(me + steps + CHIPS, CHIPS)

    barrier = pltpu.get_barrier_semaphore()

    @pl.loop(1, CHIPS)
    def _(i):
        pl.semaphore_signal(
            barrier, inc=1, device_id=(2 * chip(i) + core, tp), device_id_type=MESH
        )

    pl.semaphore_signal(barrier, inc=1, device_id=sibling, device_id_type=MESH)
    pl.semaphore_wait(barrier, CHIPS)

    def outbound(to, image, part):
        size = IMAGE_HALF if image else TEXT_HALF
        at = pl.multiple_of((2 * lax.div(to, HEADS) + part) * size, 16)
        return pay_ref.at[lax.rem(to, HEADS), :, pl.ds(at, size)]

    def landing(source, image, part):
        if image:
            at = TEXT_CHIPS * TEXT_HALF + (source - TEXT_CHIPS) * IMAGE_HALF
            size = IMAGE_HALF
        else:
            at = source * TEXT_HALF
            size = TEXT_HALF
        return pl.ds(pl.multiple_of(at, 16), size)

    def send(src, dst, send_sem, recv_sem, to):
        return pltpu.make_async_remote_copy(
            src_ref=src, dst_ref=dst, send_sem=send_sem, recv_sem=recv_sem,
            device_id=(2 * to + core, tp), device_id_type=MESH,
        )

    def both(test, do):
        @pl.when(test)
        def _():
            do(True)

        @pl.when(jnp.logical_not(test))
        def _():
            do(False)

    def start_self(image):
        for part in range(2):
            pltpu.make_async_copy(
                outbound(me, image, part),
                held.at[:, part, core, landing(me, image, part)],
                a_recv.at[me],
            ).start()

    both(is_image, start_self)

    def far_first(i):
        return lax.rem(z + ZS // 2 + lax.div(i, 2) - lax.rem(i, 2) * (1 + 2 * lax.div(i, 2)), ZS)

    @pl.loop(0, ZS - 1)
    def _(i):
        zz = far_first(i)

        def start(image):
            size = IMAGE_HALF if image else TEXT_HALF
            for part in range(2):
                to = x * ZS + zz
                send(
                    outbound(to, image, part), held.at[:, part, core, landing(me, image, part)],
                    a_send.at[0, zz], a_recv.at[me], to,
                ).start()
            for dx in (1, 3, 2):
                to = lax.rem(x + dx, XS) * ZS + z
                rows = pl.ds(
                    pl.multiple_of(
                        2 * lax.div(lax.rem(x + dx, XS) * ZS + zz, HEADS) * size, 16
                    ),
                    2 * size,
                )
                send(
                    pay_ref.at[lax.rem(zz, HEADS), :, rows],
                    relay.at[x, zz, :, pl.ds(0, 2 * size)],
                    a_send.at[dx, zz], r_recv.at[x, zz], to,
                ).start()

        both(is_image, start)

    def start_flat(image):
        for dx in (1, 3, 2):
            to = lax.rem(x + dx, XS) * ZS + z
            for part in range(2):
                send(
                    outbound(to, image, part), held.at[:, part, core, landing(me, image, part)],
                    a_send.at[dx, z], a_recv.at[me], to,
                ).start()

    both(is_image, start_flat)

    @pl.when(jnp.logical_not(is_image))
    def _():
        blank[...] = jnp.zeros_like(blank)
        pltpu.make_async_copy(blank, out_ref.at[pl.ds(TEXT_ROWS, ROWS - TEXT_ROWS)], zero_sem).start()

    starts = start_row(lengths_ref)

    @pl.loop(0, 2)
    def _(part):
        down = lax.broadcasted_iota(jnp.int32, (128, 128), 0)
        right = lax.broadcasted_iota(jnp.int32, (128, 128), 1)
        row = kpos_ref[part, core]
        for k in range(PART // 128):
            at = slice(k * 128, k * 128 + 128)
            token = jnp.sum(jnp.where(down == right, row[:, at], 0.0), axis=1, keepdims=True)
            qpos_ref[part, at, :] = token
            qstart_ref[part, at, :] = start_of(token, starts)

    def await_rows(image, sem):
        whole = pay_ref.at[0, :, pl.ds(0, 2 * (IMAGE_HALF if image else TEXT_HALF))]
        pltpu.make_async_copy(whole, whole, sem).wait()

    @pl.loop(0, ZS - 1)
    def _(i):
        zz = far_first(i)
        for dx in (1, 3, 2):
            from_x = lax.rem(x + XS - dx, XS)

            def forward(image):
                size = IMAGE_HALF if image else TEXT_HALF
                await_rows(image, r_recv.at[from_x, zz])
                source = from_x * ZS + z
                for part in range(2):
                    send(
                        relay.at[from_x, zz, :, pl.ds(part * size, size)],
                        held.at[:, part, core, landing(source, image, part)],
                        r_send.at[from_x, zz], a_recv.at[source], x * ZS + zz,
                    ).start()

            both(from_x >= XS // 2, forward)

    @pl.loop(0, CHIPS)
    def _(i):
        source = chip(-i)

        def arrive(image):
            size = 2 * (IMAGE_HALF if image else TEXT_HALF)
            whole = pay_ref.at[0, :, pl.ds(0, size)]
            pltpu.make_async_copy(whole, whole, a_recv.at[source]).wait()

        both(source >= TEXT_CHIPS, arrive)

    def share(part):
        mine = held.at[pl.ds(1, 2), part, core]
        return pltpu.make_async_remote_copy(
            src_ref=mine, dst_ref=mine, send_sem=s_send.at[part], recv_sem=s_recv.at[part],
            device_id=sibling, device_id_type=MESH,
        )

    def shared(part):
        other = held.at[pl.ds(1, 2), part, 1 - core]
        return pltpu.make_async_remote_copy(
            src_ref=other, dst_ref=other, send_sem=s_send.at[part], recv_sem=s_recv.at[part],
            device_id=sibling, device_id_type=MESH,
        )

    share(0).start()
    share(1).start()

    tiles = PART // Q_TILE

    def attend(part, side, first):
        @pl.loop(0, tiles)
        def _(tile):
            at = pl.ds(pl.multiple_of(tile * Q_TILE, Q_TILE), Q_TILE)
            query = held[0, part, core, at, :]
            place = qpos_ref[part, at, :]
            start = qstart_ref[part, at, :]
            for key_part in range(part + 1):
                keys = held[1, key_part, side]
                values = held[2, key_part, side]
                scores = lax.dot_general(
                    query, keys, (((1,), (1,)), ((), ())), preferred_element_type=jnp.float32
                )
                spots = kpos_ref[key_part, side]
                visible = spots >= start
                if key_part == part:
                    visible = visible & (spots <= place)
                weight = jnp.where(visible, jnp.exp(scores * (1.0 / math.sqrt(HD))), 0.0)
                total = jnp.sum(weight, axis=1, keepdims=True)
                product = jnp.dot(
                    weight.astype(jnp.bfloat16), values, preferred_element_type=jnp.float32
                )
                if first and key_part == 0:
                    num[part, at, :] = product
                    den[part, at, :] = jnp.broadcast_to(total, product.shape)
                else:
                    num[part, at, :] += product
                    den[part, at, :] += jnp.broadcast_to(total, product.shape)

    def finish(part):
        @pl.loop(0, tiles)
        def _(tile):
            at = pl.ds(pl.multiple_of(tile * Q_TILE, Q_TILE), Q_TILE)
            mixed[part, at, :] = (num[part, at, :] / den[part, at, :]).astype(jnp.bfloat16)

    def home(image, part):
        size = IMAGE_HALF if image else TEXT_HALF
        at = pl.multiple_of((2 * seq + part) * size, 16)
        return out_ref.at[pl.ds(at, size), pl.ds(pl.multiple_of(head * HD, HD), HD)]

    def send_home(part):
        @pl.loop(1, CHIPS)
        def _(i):
            to = chip(i)

            def start(image):
                send(
                    mixed.at[part, landing(to, image, part)], home(image, part),
                    b_send.at[part, to], b_recv.at[part, me], to,
                ).start()

            both(to >= TEXT_CHIPS, start)

        def stay(image):
            pltpu.make_async_copy(
                mixed.at[part, landing(me, image, part)], home(image, part), b_recv.at[part, me]
            ).start()

        both(is_image, stay)

    def await_mixed(image, sem):
        whole = mixed.at[0, pl.ds(0, IMAGE_HALF if image else TEXT_HALF)]
        pltpu.make_async_copy(whole, whole, sem).wait()

    for part in range(2):
        attend(part, core, True)
        shared(part).wait_recv()
        attend(part, 1 - core, False)
        finish(part)
        send_home(part)

    @pl.loop(0, CHIPS)
    def _(i):
        source = chip(-i)
        for part in range(2):
            both(is_image, lambda image: await_mixed(image, b_recv.at[part, source]))

    @pl.loop(1, CHIPS)
    def _(i):
        to = chip(i)
        for part in range(2):
            both(to >= TEXT_CHIPS, lambda image: await_mixed(image, b_send.at[part, to]))

    share(0).wait_send()
    share(1).wait_send()

    def sent(image):
        @pl.loop(0, ZS)
        def _(zz):
            for dx in range(XS):

                @pl.when(jnp.logical_or(zz != z, dx != 0))
                def _():
                    await_rows(image, a_send.at[dx, zz])

    both(is_image, sent)

    @pl.loop(1, ZS)
    def _(i):
        for dx in range(1, XS):
            from_x = lax.rem(x + dx, XS)

            def relayed(image):
                await_rows(image, r_send.at[from_x, lax.rem(z + i, ZS)])

            both(from_x >= XS // 2, relayed)

    @pl.when(jnp.logical_not(is_image))
    def _():
        pltpu.make_async_copy(blank, out_ref.at[pl.ds(TEXT_ROWS, ROWS - TEXT_ROWS)], zero_sem).wait()


def attend_all(lengths, payload, places):
    vmem = pl.BlockSpec(memory_space=pltpu.VMEM)
    dma = pltpu.SemaphoreType.DMA
    return pl.pallas_call(
        attend_kernel,
        name="exchange_attend",
        out_shape=jax.ShapeDtypeStruct((ROWS, WIDTH), jnp.bfloat16),
        in_specs=[pl.BlockSpec(memory_space=pltpu.SMEM), vmem, vmem],
        out_specs=pl.BlockSpec(memory_space=pl.ANY),
        scratch_shapes=[
            pltpu.VMEM((3, 2, 2, PART, HD), jnp.bfloat16),
            pltpu.VMEM((XS, ZS, 3, 2 * IMAGE_HALF, HD), jnp.bfloat16),
            pltpu.VMEM((2, PART, 1), jnp.float32),
            pltpu.VMEM((2, PART, 1), jnp.float32),
            pltpu.VMEM((2, PART, HD), jnp.float32),
            pltpu.VMEM((2, PART, HD), jnp.float32),
            pltpu.VMEM((2, PART, HD), jnp.bfloat16),
            pltpu.VMEM((ROWS - TEXT_ROWS, WIDTH), jnp.bfloat16),
            dma((XS, ZS)), dma((CHIPS,)),
            dma((XS, ZS)), dma((XS, ZS)),
            dma((2,)), dma((2,)),
            dma((2, CHIPS)), dma((2, CHIPS)),
            dma,
        ],
        compiler_params=pltpu.CompilerParams(
            collective_id=1, has_side_effects=True, vmem_limit_bytes=60 << 20
        ),
    )(lengths, payload, places)


def arrival_codes():
    codes = np.zeros((8, PART), np.float32)
    at = 0
    for chip in range(CHIPS):
        each = 2 if chip < TEXT_CHIPS else 6
        for block in range(8):
            for rank in range(each):
                codes[:4, at] = (2 * chip, 2 * chip + 1, rank, block)
                at += 1
    return codes


def on_device(stream, norm_gain, qkv_weight, qk_gain, owner, doc_lengths):
    half = np.arange(HD) % (HD // 2)
    freqs = np.exp(-math.log(rope_base) * 2.0 * half / HD).astype(np.float32)[None, :]
    lengths = jnp.transpose(doc_lengths)
    payload, places = project(
        lengths, jnp.transpose(qkv_weight, (0, 2, 1, 3)), stream, norm_gain, qk_gain,
        owner.reshape(2 * BLOCKS, BLOCK // 2), jnp.asarray(freqs), jnp.asarray(arrival_codes()),
    )
    return attend_all(lengths, payload, places)


def solution(mesh):
    return jax.shard_map(
        on_device,
        mesh=mesh,
        in_specs=(P("mod", None), P(), P(None, "mod", None, "tp"), P(None, None, "tp"), P(), P()),
        out_specs=P("mod", "tp"),
        check_vma=False,
    )
```
